128 devices in a mesh: lat: 8 (over x, core), lon: 16 (over z, y).
Axes of the slice: x: 4, y: 4, z: 4, core: 2. Of those that a mesh axis runs over, the one named last changes fastest.
Arguments:
- adjoint_in: bfloat16 [256, 64, 4096], P(None, 'lat', 'lon'), may hold values from -6 to 6
- layer_input: bfloat16 [256, 64, 4096], P(None, 'lat', 'lon'), may hold values from -6 to 6
- conv_weight: bfloat16 [8, 9, 32, 32], replicated, may hold values from -0.375 to 0.375
- footprint: int32 [2048, 64], P(('lat', 'lon')), may hold values from 0 to 262143, as said below
- owner: int32 [2048, 1], P(('lat', 'lon')), may hold values from 0 to 15; in each aligned block of 16 rows (0 to 15, 16 to 31, ...) at most 2 rows name the same one
- obs_weight: bfloat16 [4096, 32, 64], P(('lat', 'lon')), may hold values from -0.75 to 0.75
- obs_value: bfloat16 [4096, 32, 256], P(('lat', 'lon')), may hold values from -6 to 6
- obs_precision: bfloat16 [4096, 256], P(('lat', 'lon')), may hold values from 0.25 to 4
- obs_count: int32 [4096], P(('lat', 'lon')), may hold values from 1 to 32
Outputs:
- adjoint_out: bfloat16 [256, 64, 4096], P(None, 'lat', 'lon')
- weight_grad: float32 [8, 9, 32, 32], replicated
The draws below stay inside these ranges and needn't reach their ends.
Inputs may be any that keep to these rules, and one draw needn't show every extreme that they name: `footprint`: the cells of one track form a 8 x 8 square of the grid lying inside the block of cells of the device that holds the track. Among the 16 tracks of one device no owner is named more than 2 times.
All inputs are finite; a program needn't handle non-finite values.
Results may differ from the reference program's by a relative error of at most 0.0045.
Values may be sent and summed in bfloat16 or wider, within the bound.
A program may use at most 128 MiB of HBM per device.

```python
import math
import jax
import jax.numpy as jnp
import numpy as np
from jax import lax

C = 256
GROUP = 32
GROUPS = 8
HLAT = 8
HLON = 256
PATCH = 8
P_SIZE = 64
K = 32
TRK_DEV = 16
CAP = 2
NLAT = 64
NLON = 4096
TRACKS = 2048
INBOX = 4096
N_LAT = 8
N_LON = 16


def draw_footprint(key, part):
    row_key, col_key = jax.random.split(key)
    tracks = TRK_DEV * N_LAT * N_LON
    row_corner = jax.random.randint(row_key, (tracks,), 0, HLAT - PATCH + 1)
    col_corner = jax.random.randint(col_key, (tracks,), 0, HLON - PATCH + 1)
    row_corner = row_corner.at[0].set(0).at[tracks - 1].set(HLAT - PATCH)
    col_corner = col_corner.at[0].set(0).at[tracks - 1].set(HLON - PATCH)
    device = jnp.arange(tracks, dtype=jnp.int32) // TRK_DEV
    lat_cell = device // N_LON * HLAT + row_corner
    lon_cell = device % N_LON * HLON + col_corner
    offsets = jnp.arange(PATCH * PATCH, dtype=jnp.int32)
    lat_all = lat_cell[:, None] + offsets[None, :] // PATCH
    lon_all = lon_cell[:, None] + offsets[None, :] % PATCH
    return (lat_all * NLON + lon_all).astype(jnp.int32)


def with_ends(values, key, least, high):
    index_at = [jax.random.randint(jax.random.fold_in(key, axis), (), 0, length) for axis, length in enumerate(values.shape)]
    main_axis = values.shape.index(max(values.shape))
    next_to = index_at[:main_axis] + [(index_at[main_axis] + 1) % values.shape[main_axis]] + index_at[main_axis + 1:]
    return values.at[tuple(index_at)].set(least).at[tuple(next_to)].set(high)


def steps_of(own_key, dims, shards, least, largest):
    level, own = 1.0, jax.random.fold_in(own_key, 6)
    for dim, shards_of in shards:
        steps = jnp.exp(jax.random.uniform(jax.random.fold_in(own, dim), (shards_of,), jnp.float32, least / len(shards), largest / len(shards)))
        level = level * jnp.repeat(steps, dims[dim] // shards_of).reshape([-1 if axis == dim else 1 for axis in range(len(dims))])
    return level


def shared_out(rng, own, number, rows, count, top, limit, skew):
    ranking = jax.random.permutation(rng, count)
    heavy_load, ordinary = portions_of(count, rows * top, limit, skew, True), portions_of(count, rows * top, limit, skew, False)
    places = jnp.arange(count)

    def named(lengths, turn):
        used = int((lengths > 0).sum())
        fixed = max(1, used // 4)
        moved = fixed + (places - fixed + turn * (used - fixed)) % max(1, count - fixed)
        return jnp.zeros((count,), jnp.int32).at[ranking[jnp.where(places < fixed, places, moved)]].set(jnp.asarray(lengths, jnp.int32))

    lengths = jnp.where(number % 4 == 0, named(heavy_load, number // 4), named(ordinary, number - number // 4 - 1))
    mixed = jax.random.permutation(jax.random.fold_in(own, 3), count)
    source_of, sink = mixed[0:count // 2 * 2:2], mixed[1:count // 2 * 2:2]
    margin = jnp.minimum(lengths[source_of] - 1, limit - lengths[sink]) // 2
    margin = jnp.where((source_of == ranking[0]) | (sink == ranking[0]) | (lengths[sink] == 0), 0, jnp.maximum(margin, 0))
    moved = jax.random.randint(jax.random.fold_in(own, 4), (count // 2,), 0, 1 << 20) % (margin + 1)
    lengths = lengths.at[source_of].add(-moved).at[sink].add(moved)
    items = jnp.searchsorted(jnp.cumsum(lengths), jnp.arange(rows * top), side="right").astype(jnp.int32)
    grid = items.reshape(top, rows).T
    grid = grid[jax.random.permutation(jax.random.fold_in(own, 1), rows)]
    turn = jax.random.randint(jax.random.fold_in(own, 2), (rows, 1), 0, top)
    return jnp.take_along_axis(grid, (jnp.arange(top)[None, :] + turn) % top, axis=1)


def portions_of(number_of, total, reach, slope, full):
    portions = [(1 << 20) // math.isqrt(standing ** slope) + 1 for standing in range(1, number_of + 1)]
    largest = reach if full else min(reach, max(-(-total // number_of), total * portions[0] // sum(portions)))
    least = 1 if total - largest >= number_of - 1 else 0
    holding, spare = [largest] + [least] * (number_of - 1), total - largest - least * (number_of - 1)
    while spare > 0:
        candidates = [i for i in range(1, number_of) if holding[i] < largest] or [i for i in range(1, number_of) if holding[i] < reach]
        mass, budget = sum([portions[i] for i in candidates]), spare
        for i in candidates:
            extra = min(reach - holding[i], max(1, budget * portions[i] // mass), spare)
            holding[i] = holding[i] + extra
            spare = spare - extra
    return np.array(holding)


def gaussian(stream_key, dims, spread, reach, pieces=(), held_as=jnp.bfloat16):
    result = jax.random.normal(stream_key, dims, jnp.float32) * spread
    if len(pieces) > 0:
        result = steps_of(stream_key, dims, pieces, -0.22, 0.18) * result
    return jnp.clip(result, min=-reach, max=reach).astype(held_as)


def setup_inputs(seed: int = 0) -> dict:
    key_list = jax.random.split(jax.random.key(seed), 10)
    adjoint_in = gaussian(key_list[0], (C, NLAT, NLON), 1.0, 6.0, ((1, 8), (2, 16)))
    layer_input = gaussian(key_list[1], (C, NLAT, NLON), 1.0, 6.0, ((1, 8), (2, 16)))
    conv_weight = gaussian(key_list[2], (GROUPS, 9, GROUP, GROUP), (9 * GROUP) ** -0.5, 0.375)
    footprint = draw_footprint(jax.random.fold_in(key_list[9], 71), 0)
    owner_keys = jax.random.split(jax.random.fold_in(key_list[4], 1), TRACKS // TRK_DEV)
    owner_turns = jax.random.permutation(jax.random.fold_in(key_list[4], 3), TRACKS // TRK_DEV)
    owner = jax.vmap(lambda own, number: shared_out(jax.random.fold_in(key_list[4], 2), own, number, TRK_DEV, N_LON, 1, CAP, 2))(owner_keys, owner_turns).reshape((TRACKS, 1))
    obs_weight = gaussian(key_list[5], (INBOX, K, P_SIZE), P_SIZE ** -0.5, 0.75, ((0, 128),))
    obs_value = gaussian(key_list[6], (INBOX, K, C), 1.0, 6.0, ((0, 128),))
    obs_precision = jnp.clip(jnp.exp(math.log(4.0) - 2.7725887 * jax.random.uniform(key_list[7], (INBOX, C), jnp.float32) ** steps_of(key_list[7], (INBOX, C), ((0, 128),), -0.2, 0.2)), 0.25, 4.0).astype(jnp.bfloat16)
    obs_count = with_ends(jax.random.randint(key_list[8], (INBOX,), 1, K + 1), jax.random.fold_in(key_list[8], 1), 1, K).astype(jnp.int32)
    return dict(adjoint_in=adjoint_in, layer_input=layer_input, conv_weight=conv_weight, footprint=footprint, owner=owner, obs_weight=obs_weight, obs_value=obs_value, obs_precision=obs_precision, obs_count=obs_count)


def wrap_pad(source_field):
    widths = [(0, 0)] * (source_field.ndim - 2) + [(2, 2), (0, 0)]
    padded = jnp.pad(source_field, widths)
    return jnp.concatenate([padded[..., -2:], padded, padded[..., :2]], axis=-1)

def reference(adjoint_in, layer_input, conv_weight, footprint, owner, obs_weight, obs_value, obs_precision, obs_count):
    groups = C // GROUP
    adjoint_groups = adjoint_in.reshape(groups, GROUP, NLAT, NLON)
    input_groups = layer_input.reshape(groups, GROUP, NLAT, NLON)

    def one_group(operands):
        adjoint_group, input_group, weight_group = operands
        adjoint_f = adjoint_group.astype(jnp.float32)
        adjoint_pad = wrap_pad(adjoint_f)
        input_pad = wrap_pad(input_group.astype(jnp.float32))
        weight_f = weight_group.astype(jnp.float32)
        backward = jnp.zeros((GROUP, NLAT, NLON), jnp.float32)
        tap_grads = []
        for row_tap in range(3):
            for col_tap in range(3):
                tap_index = 3 * row_tap + col_tap
                shifted = adjoint_pad[:, 4 - 2 * row_tap:4 - 2 * row_tap + NLAT, 4 - 2 * col_tap:4 - 2 * col_tap + NLON]
                backward = backward + jnp.einsum('io,ohw->ihw', weight_f[tap_index], shifted)
                moved_input = input_pad[:, 2 * row_tap:2 * row_tap + NLAT, 2 * col_tap:2 * col_tap + NLON]
                tap_grads.append(jnp.einsum('ihw,ohw->io', moved_input, adjoint_f))
        return (backward, jnp.stack(tap_grads))
    backward, weight_grad = lax.map(one_group, (adjoint_groups, input_groups, conv_weight))
    weight_grad = weight_grad * (1.0 / math.sqrt(NLAT * NLON))
    devices = N_LAT * N_LON
    target = owner[:, 0].reshape(devices, TRK_DEV)
    onehot = (target[:, :, None] == jnp.arange(N_LON, dtype=jnp.int32)[None, None, :]).astype(jnp.int32)
    position = lax.optimization_barrier(jnp.sum((jnp.cumsum(onehot, axis=1) - onehot) * onehot, axis=2))
    device = jnp.arange(devices, dtype=jnp.int32)[:, None]
    lat_band = device // N_LON
    lon_band = device % N_LON
    inbox_row = (((lat_band * N_LON + target) * N_LON + lon_band) * CAP + position).reshape(-1).astype(jnp.int32)
    live_rows = jnp.arange(K, dtype=jnp.int32)[None, :] < obs_count[inbox_row][:, None]
    picked = obs_weight[inbox_row]
    wmask = jnp.where(live_rows[:, :, None], picked, jnp.zeros_like(picked)).astype(jnp.float32)
    flattened = layer_input.reshape(C, NLAT * NLON)
    values = jnp.transpose(flattened[:, footprint], (1, 2, 0)).astype(jnp.float32)
    model_obs = jnp.einsum('tkp,tpc->tkc', wmask, values)
    misfit = ((model_obs - obs_value[inbox_row].astype(jnp.float32)) * obs_precision[inbox_row].astype(jnp.float32)[:, None, :]).astype(jnp.bfloat16)
    pulled = jnp.einsum('tkp,tkc->tpc', wmask, misfit.astype(jnp.float32)).astype(jnp.bfloat16)
    pulled = lax.optimization_barrier(pulled).astype(jnp.float32)
    obs_field = jnp.zeros((C, NLAT * NLON), jnp.float32).at[:, footprint.reshape(-1)].add(pulled.reshape(-1, C).T)
    total = adjoint_in.astype(jnp.float32) + backward.reshape(C, NLAT, NLON) + obs_field.reshape(C, NLAT, NLON)
    return (total.astype(jnp.bfloat16), weight_grad)
```

```python
import math

import jax
import jax.numpy as jnp
from jax import lax
from jax.experimental import pallas as pl
from jax.experimental.pallas import tpu as pltpu
from jax.sharding import PartitionSpec as P

MESH = pl.DeviceIdType.MESH
N_LAT = 8
N_LON = 16
CH = 256
ROWS = 8
COLS = 256
CELLS = ROWS * COLS
PAD = 16
GROUP = 32
TRACKS = 16
K = 32
PTS = 64
CHUNK = 40
F32 = jnp.float32
BF16 = jnp.bfloat16
NT = (((1,), (1,)), ((), ()))


def iota(shape, dim):
    return lax.broadcasted_iota(jnp.int32, shape, dim)


def kernel(
    owner,
    cell,
    adj_t,
    x_in,
    conv_w,
    obs_w,
    obs_v,
    obs_pc,
    out,
    grad_out,
    ext,
    shifted,
    x_nat,
    x_f32,
    x_mat,
    w_in,
    w_diag,
    blocks,
    obs_op,
    misfit,
    w_buf,
    v_buf,
    pc_buf,
    grad,
    rs_buf,
    part,
    ex_buf,
    gathered,
    local_sem,
    halo_send,
    halo_recv,
    obs_send,
    obs_recv,
    rs_send,
    rs_recv,
    ex_send,
    ex_recv,
    ag_send,
    ag_recv,
):
    lat = lax.axis_index("lat")
    lon = lax.axis_index("lon")
    north = lax.rem(lat + N_LAT - 1, N_LAT)
    south = lax.rem(lat + 1, N_LAT)
    west = lax.rem(lon + N_LON - 1, N_LON)
    east = lax.rem(lon + 1, N_LON)

    local = [
        pltpu.make_async_copy(x_in, x_nat, local_sem.at[0]),
        pltpu.make_async_copy(conv_w, w_in, local_sem.at[1]),
        pltpu.make_async_copy(
            adj_t, ext.at[pl.ds(2, ROWS), pl.ds(PAD, COLS), :], local_sem.at[2]
        ),
        pltpu.make_async_copy(obs_w.at[lon], w_buf.at[lon], local_sem.at[3]),
        pltpu.make_async_copy(obs_v.at[lon], v_buf.at[lon], local_sem.at[4]),
        pltpu.make_async_copy(obs_pc.at[lon], pc_buf.at[lon], local_sem.at[5]),
    ]
    for copy in local:
        copy.start()

    barrier = pltpu.get_barrier_semaphore()

    def greet(to_lat, to_lon):
        pl.semaphore_signal(barrier, inc=1, device_id=(to_lat, to_lon), device_id_type=MESH)

    for to_lat, to_lon in ((north, west), (north, east), (south, west), (south, east)):
        greet(to_lat, to_lon)
    for k in range(1, N_LAT):
        greet(lax.rem(lat + k, N_LAT), lon)
    for k in range(1, N_LON):
        greet(lat, lax.rem(lon + k, N_LON))

    local[0].wait()
    for half in range(2):
        x_f32[half] = (
            x_nat[:, :, 128 * half : 128 * half + 128].astype(F32).reshape(CELLS, 128)
        )
    for i in range(ROWS):
        for half in range(2):
            at = COLS * i + 128 * half
            x_mat[:, at : at + 128] = x_f32[half, pl.ds(i, CH, stride=ROWS), :].astype(BF16)

    pl.semaphore_wait(barrier, 4 + N_LAT - 1 + N_LON - 1)

    def halo(index, rows, cols, to_rows, to_cols, to_lat, to_lon):
        return pltpu.make_async_remote_copy(
            src_ref=adj_t.at[pl.ds(*rows), pl.ds(*cols), :],
            dst_ref=ext.at[pl.ds(*to_rows), pl.ds(*to_cols), :],
            send_sem=halo_send.at[index],
            recv_sem=halo_recv.at[index],
            device_id=(to_lat, to_lon),
            device_id_type=MESH,
        )

    first_rows, last_rows, all_rows = (0, 2), (ROWS - 2, 2), (0, ROWS)
    first_cols, last_cols, all_cols = (0, PAD), (COLS - PAD, PAD), (0, COLS)
    top, bottom, middle = (0, 2), (ROWS + 2, 2), (2, ROWS)
    left, right, centre = (0, PAD), (COLS + PAD, PAD), (PAD, COLS)
    halos = [
        halo(0, all_rows, last_cols, middle, left, lat, east),
        halo(1, all_rows, first_cols, middle, right, lat, west),
        halo(2, last_rows, last_cols, top, left, south, east),
        halo(3, last_rows, first_cols, top, right, south, west),
        halo(4, first_rows, last_cols, bottom, left, north, east),
        halo(5, first_rows, first_cols, bottom, right, north, west),
        halo(6, last_rows, all_cols, top, centre, south, lon),
        halo(7, first_rows, all_cols, bottom, centre, north, lon),
    ]
    for copy in halos:
        copy.start()

    def obs_copies(k):
        peer = lax.rem(lon + k, N_LON)
        return [
            pltpu.make_async_remote_copy(
                src_ref=src.at[peer],
                dst_ref=dst.at[lon],
                send_sem=obs_send.at[index, k],
                recv_sem=obs_recv.at[index, k],
                device_id=(lat, peer),
                device_id_type=MESH,
            )
            for index, (src, dst) in enumerate(
                ((obs_w, w_buf), (obs_v, v_buf), (obs_pc, pc_buf))
            )
        ]

    def start_obs(k, carry):
        for copy in obs_copies(k):
            copy.start()
        return carry

    lax.fori_loop(1, N_LON, start_obs, 0)

    local[1].wait()
    spread = (iota((CH, GROUP), 0) % GROUP == iota((CH, GROUP), 1)).astype(F32).astype(BF16)
    same_group = iota((CH, CH), 0) // GROUP == iota((CH, CH), 1) // GROUP
    for tap in range(9):
        stacked = jnp.concatenate([w_in[g, tap] for g in range(CH // GROUP)], axis=0)
        tiled = lax.dot_general(spread, stacked, NT, preferred_element_type=F32)
        w_diag[tap] = jnp.where(same_group, tiled, 0.0).astype(BF16)

    local[2].wait()
    scale = 1.0 / math.sqrt(CELLS * N_LAT * N_LON)
    lane_group = iota((GROUP, 128), 1) // GROUP

    def add_grad(tap, x_from, rows, read, fresh):
        product = jnp.dot(
            x_mat[:, COLS * x_from : COLS * (x_from + rows)],
            read.reshape(rows * COLS, CH),
            preferred_element_type=F32,
        )
        for half in range(2):
            value = jnp.zeros((GROUP, 128), F32)
            for q in range(4):
                g = 4 * half + q
                block = product[g * GROUP : (g + 1) * GROUP, 128 * half : 128 * half + 128]
                value = jnp.where(lane_group == q, block, value)
            value = value * scale
            at = pl.ds(tap * 64 + half * GROUP, GROUP)
            grad[at, :] = value if fresh else grad[at, :] + value

    inner = ((0, 0, 6, 4), (1, 0, 8, 2), (2, 2, 6, 2))
    for a, x_from, rows, row in inner:
        add_grad(
            3 * a + 1, x_from, rows, ext[row : row + rows, PAD : PAD + COLS, :], True
        )

    def shift_row(row):
        shifted[0, row] = ext[row, pl.ds(PAD + 2, COLS), :]
        shifted[1, row] = ext[row, pl.ds(PAD - 2, COLS), :]

    halos[0].wait_recv()
    halos[1].wait_recv()

    def shift_inner(row, carry):
        shift_row(row)
        return carry

    lax.fori_loop(2, ROWS + 2, shift_inner, 0)
    for a, x_from, rows, row in inner:
        for b in (0, 2):
            add_grad(3 * a + b, x_from, rows, shifted[b // 2, row : row + rows], True)

    for copy in halos[2:]:
        copy.wait_recv()

    @pl.when(lat == 0)
    def _():
        ext[0:2] = jnp.zeros((2, COLS + 2 * PAD, CH), BF16)

    @pl.when(lat == N_LAT - 1)
    def _():
        ext[ROWS + 2 : ROWS + 4] = jnp.zeros((2, COLS + 2 * PAD, CH), BF16)

    for row in (0, 1, ROWS + 2, ROWS + 3):
        shift_row(row)
    for a, x_from, row in ((0, 6, 10), (2, 0, 0)):
        add_grad(3 * a + 1, x_from, 2, ext[row : row + 2, PAD : PAD + COLS, :], False)
        for b in (0, 2):
            add_grad(3 * a + b, x_from, 2, shifted[b // 2, row : row + 2], False)
    grad[576:640, :] = jnp.zeros((64, 128), F32)

    def rs_copy(k):
        peer = lax.rem(lon + k, N_LON)
        return pltpu.make_async_remote_copy(
            src_ref=grad.at[pl.ds(pl.multiple_of(CHUNK * peer, 8), CHUNK), :],
            dst_ref=rs_buf.at[k],
            send_sem=rs_send.at[k],
            recv_sem=rs_recv.at[k],
            device_id=(lat, peer),
            device_id_type=MESH,
        )

    def start_rs(k, carry):
        rs_copy(k).start()
        return carry

    lax.fori_loop(1, N_LON, start_rs, 0)

    for copy in local[3:]:
        copy.wait()

    def wait_obs(k, carry):
        for copy in obs_copies(k):
            copy.wait_recv()
        return carry

    lax.fori_loop(1, N_LON, wait_obs, 0)
    owners = [owner[t] for t in range(TRACKS)]
    places = [
        jnp.minimum(
            sum([(owners[u] == owners[t]).astype(jnp.int32) for u in range(t)], jnp.int32(0)), 1
        )
        for t in range(TRACKS)
    ]
    widen = (iota((PTS, 4 * PTS), 1) % PTS == iota((PTS, 4 * PTS), 0)).astype(F32).astype(BF16)
    same_track = iota((4 * K, 4 * PTS), 0) // K == iota((4 * K, 4 * PTS), 1) // PTS
    obs_row = iota((K, PTS), 0).astype(F32)
    for q in range(4):
        picked = []
        for t in range(4 * q, 4 * q + 4):
            weight = w_buf[owners[t], places[t]]
            count = pc_buf[owners[t], places[t]][1:2, :PTS].astype(F32)
            picked.append(jnp.where(obs_row < count, weight.astype(F32), 0.0))
        stacked = jnp.concatenate(picked, axis=0).astype(BF16)
        tiled = jnp.dot(stacked, widen, preferred_element_type=F32)
        blocks[q] = jnp.where(same_track, tiled, 0.0).astype(BF16)

    def build_op(i, carry):
        here = iota((COLS, 4 * PTS), 0) + i * COLS
        at = pl.ds(pl.multiple_of(i * COLS, COLS), COLS)
        for q in range(4):
            hit = jnp.where(here == cell[q : q + 1, :], 1.0, 0.0).astype(BF16)
            obs_op[at, 4 * K * q : 4 * K * (q + 1)] = lax.dot_general(
                hit, blocks[q], NT, preferred_element_type=F32
            ).astype(BF16)
        return carry

    lax.fori_loop(0, ROWS, build_op, 0)
    model_obs = jnp.dot(x_mat[...], obs_op[...], preferred_element_type=F32).T
    for t in range(TRACKS):
        at = slice(K * t, K * (t + 1))
        value = v_buf[owners[t], places[t]].astype(F32)
        precision = pc_buf[owners[t], places[t]][0:1, :].astype(F32)
        misfit[at, :] = ((model_obs[at, :] - value) * precision).astype(BF16)

    def finish_rows(first, last):
        def one(i, carry):
            total = ext[i + 2, PAD : PAD + COLS, :].astype(F32)
            for a in range(3):
                row = i + 4 - 2 * a
                taps = (
                    shifted[0, row],
                    ext[row, PAD : PAD + COLS, :],
                    shifted[1, row],
                )
                for b in range(3):
                    total += jnp.dot(
                        taps[b], w_diag[3 * a + b], preferred_element_type=F32
                    )
            at = pl.ds(pl.multiple_of(i * COLS, COLS), COLS)
            total += jnp.dot(obs_op[at, :], misfit[...], preferred_element_type=F32)
            out[i] = total.astype(BF16)
            return carry

        lax.fori_loop(first, last, one, 0)

    def wait_rs(k, carry):
        rs_copy(k).wait_recv()
        return carry

    lax.fori_loop(1, N_LON, wait_rs, 0)
    own = grad[pl.ds(pl.multiple_of(CHUNK * lon, 8), CHUNK), :]
    for k in range(1, N_LON):
        own += rs_buf[k]
    part[...] = own
    ex_buf[lat] = own

    def ex_copy(k):
        return pltpu.make_async_remote_copy(
            src_ref=part,
            dst_ref=ex_buf.at[lat],
            send_sem=ex_send.at[k],
            recv_sem=ex_recv.at[k],
            device_id=(lax.rem(lat + k, N_LAT), lon),
            device_id_type=MESH,
        )

    for k in range(1, N_LAT):
        ex_copy(k).start()
    finish_rows(0, 4)
    for k in range(1, N_LAT):
        ex_copy(k).wait_recv()
    whole = ex_buf[0]
    for k in range(1, N_LAT):
        whole += ex_buf[k]
    mine = pl.ds(pl.multiple_of(CHUNK * lon, 8), CHUNK)
    gathered[mine, :] = whole

    def ag_copy(k):
        return pltpu.make_async_remote_copy(
            src_ref=gathered.at[mine, :],
            dst_ref=gathered.at[mine, :],
            send_sem=ag_send.at[k],
            recv_sem=ag_recv.at[k],
            device_id=(lat, lax.rem(lon + k, N_LON)),
            device_id_type=MESH,
        )

    def start_ag(k, carry):
        ag_copy(k).start()
        return carry

    lax.fori_loop(1, N_LON, start_ag, 0)
    finish_rows(4, 8)

    def wait_ag(k, carry):
        ag_copy(k).wait_recv()
        return carry

    lax.fori_loop(1, N_LON, wait_ag, 0)
    grad_out[...] = gathered[0:576, :]

    for copy in halos:
        copy.wait_send()

    def wait_sends(k, carry):
        for copy in obs_copies(k):
            copy.wait_send()
        rs_copy(k).wait_send()
        ag_copy(k).wait_send()
        return carry

    lax.fori_loop(1, N_LON, wait_sends, 0)
    for k in range(1, N_LAT):
        ex_copy(k).wait_send()


def on_device(
    adjoint_in,
    layer_input,
    conv_weight,
    footprint,
    owner,
    obs_weight,
    obs_value,
    obs_precision,
    obs_count,
):
    lat_start = lax.axis_index("lat") * ROWS
    lon_start = lax.axis_index("lon") * COLS
    full_width = COLS * N_LON
    cell = (footprint // full_width - lat_start) * COLS + (footprint % full_width - lon_start)
    counts = jnp.broadcast_to(obs_count[:, None], (2 * N_LON, CH)).astype(BF16)
    precision_count = jnp.stack([obs_precision, counts], axis=1).reshape(N_LON, 2, 2, CH)
    anywhere = pl.BlockSpec(memory_space=pl.ANY)
    vmem = pl.BlockSpec(memory_space=pltpu.VMEM)
    out, grad = pl.pallas_call(
        kernel,
        out_shape=(
            jax.ShapeDtypeStruct((ROWS, COLS, CH), BF16),
            jax.ShapeDtypeStruct((576, 128), F32),
        ),
        in_specs=[pl.BlockSpec(memory_space=pltpu.SMEM), vmem] + [anywhere] * 6,
        out_specs=(vmem, vmem),
        scratch_shapes=[
            pltpu.VMEM((ROWS + 4, COLS + 2 * PAD, CH), BF16),
            pltpu.VMEM((2, ROWS + 4, COLS, CH), BF16),
            pltpu.VMEM((CH, ROWS, COLS), BF16),
            pltpu.VMEM((2, CELLS, 128), F32),
            pltpu.VMEM((CH, CELLS), BF16),
            pltpu.VMEM((CH // GROUP, 9, GROUP, GROUP), BF16),
            pltpu.VMEM((9, CH, CH), BF16),
            pltpu.VMEM((4, 4 * K, 4 * PTS), BF16),
            pltpu.VMEM((CELLS, TRACKS * K), BF16),
            pltpu.VMEM((TRACKS * K, CH), BF16),
            pltpu.VMEM((N_LON, 2, K, PTS), BF16),
            pltpu.VMEM((N_LON, 2, K, CH), BF16),
            pltpu.VMEM((N_LON, 2, 2, CH), BF16),
            pltpu.VMEM((640, 128), F32),
            pltpu.VMEM((N_LON, CHUNK, 128), F32),
            pltpu.VMEM((CHUNK, 128), F32),
            pltpu.VMEM((N_LAT, CHUNK, 128), F32),
            pltpu.VMEM((640, 128), F32),
            pltpu.SemaphoreType.DMA((6,)),
            pltpu.SemaphoreType.DMA((8,)),
            pltpu.SemaphoreType.DMA((8,)),
            pltpu.SemaphoreType.DMA((3, N_LON)),
            pltpu.SemaphoreType.DMA((3, N_LON)),
            pltpu.SemaphoreType.DMA((N_LON,)),
            pltpu.SemaphoreType.DMA((N_LON,)),
            pltpu.SemaphoreType.DMA((N_LAT,)),
            pltpu.SemaphoreType.DMA((N_LAT,)),
            pltpu.SemaphoreType.DMA((N_LON,)),
            pltpu.SemaphoreType.DMA((N_LON,)),
        ],
        compiler_params=pltpu.CompilerParams(
            collective_id=0, has_side_effects=True, vmem_limit_bytes=50 * 1024 * 1024
        ),
    )(
        owner.reshape(TRACKS),
        cell.reshape(4, 4 * PTS),
        jnp.transpose(adjoint_in, (1, 2, 0)),
        layer_input,
        conv_weight,
        obs_weight.reshape(N_LON, 2, K, PTS),
        obs_value.reshape(N_LON, 2, K, CH),
        precision_count,
    )
    weight_grad = grad.reshape(9, 2, GROUP, 4, GROUP).transpose(1, 3, 0, 2, 4)
    return (
        jnp.transpose(out, (2, 0, 1)),
        weight_grad.reshape(CH // GROUP, 9, GROUP, GROUP),
    )


def solution(mesh):
    in_specs = (
        P(None, "lat", "lon"),
        P(None, "lat", "lon"),
        P(),
        P(("lat", "lon"), None),
        P(("lat", "lon"), None),
        P(("lat", "lon"), None, None),
        P(("lat", "lon"), None, None),
        P(("lat", "lon"), None),
        P(("lat", "lon")),
    )
    out_specs = (P(None, "lat", "lon"), P())
    return jax.shard_map(
        on_device, mesh=mesh, in_specs=in_specs, out_specs=out_specs, check_vma=False
    )
```

```python
import math

import jax
import jax.numpy as jnp
from jax import lax
from jax.experimental import pallas as pl
from jax.experimental.pallas import tpu as pltpu
from jax.sharding import PartitionSpec as P

MESH = pl.DeviceIdType.MESH
N_LAT = 8
N_LON = 16
CH = 256
ROWS = 8
COLS = 256
CELLS = ROWS * COLS
GROUP = 32
TRACKS = 16
K = 32
PTS = 64
CHUNK = 40
CB = 64
F32 = jnp.float32
BF16 = jnp.bfloat16
NT = (((1,), (1,)), ((), ()))


def iota(shape, dim):
    return lax.broadcasted_iota(jnp.int32, shape, dim)


def turn(value, shift):
    return pltpu.roll(value, shift % 128, 1) if shift % 128 else value


def kernel(
    owner_in,
    counts_in,
    fp_in,
    adj_in,
    x_in,
    conv_w,
    obs_w,
    obs_v,
    obs_p,
    out,
    grad_out,
    owner,
    counts,
    fp,
    a_nat,
    x_nat,
    f_buf,
    a_rows,
    a_shift,
    x_rows,
    x_edge,
    e_own,
    e_in,
    e_wide,
    halo_cols,
    a_edge,
    w_in,
    w_diag,
    obs_op,
    blocks,
    cell_row,
    w_nat,
    p_nat,
    w_own,
    p_own,
    w_buf,
    v_buf,
    p_buf,
    grad,
    g_acc,
    rs_buf,
    part,
    ex_buf,
    gathered,
    local_sem,
    halo_send,
    halo_recv,
    obs_send,
    obs_recv,
    rs_send,
    rs_recv,
    ex_send,
    ex_recv,
    ag_send,
    ag_recv,
):
    lat = lax.axis_index("lat")
    lon = lax.axis_index("lon")
    north = lax.rem(lat + N_LAT - 1, N_LAT)
    south = lax.rem(lat + 1, N_LAT)
    west = lax.rem(lon + N_LON - 1, N_LON)
    east = lax.rem(lon + 1, N_LON)

    local = [
        pltpu.make_async_copy(src, dst, local_sem.at[index])
        for index, (src, dst) in enumerate(
            (
                (adj_in, a_nat),
                (x_in, x_nat),
                (obs_w, w_nat),
                (obs_p, p_nat),
                (conv_w, w_in),
                (obs_v.at[lon], v_buf.at[lon]),
                (owner_in, owner),
                (counts_in, counts),
                (fp_in, fp),
            )
        )
    ]
    for copy in local:
        copy.start()

    barrier = pltpu.get_barrier_semaphore()

    def greet(to_lat, to_lon):
        pl.semaphore_signal(barrier, inc=1, device_id=(to_lat, to_lon), device_id_type=MESH)

    for to_lat, to_lon in ((north, west), (north, east), (south, west), (south, east)):
        greet(to_lat, to_lon)
    for k in range(1, N_LAT):
        greet(lax.rem(lat + k, N_LAT), lon)
    for k in range(1, N_LON):
        greet(lat, lax.rem(lon + k, N_LON))

    lane = iota((CB, 128), 1)

    def split_rows(native, put):
        for half in range(2):
            f_buf[half] = (
                native[:, :, 128 * half : 128 * half + 128].astype(F32).reshape(CELLS, 128)
            )
        for c in range(0, CH, CB):
            first = jnp.zeros((CB, 128), F32)
            last = jnp.zeros((CB, 128), F32)
            for i in range(ROWS):
                low = f_buf[0, pl.ds(ROWS * c + i, CB, stride=ROWS), :]
                high = f_buf[1, pl.ds(ROWS * c + i, CB, stride=ROWS), :]
                here = lane // 2 == i
                first = jnp.where(here, turn(low, 2 * i), first)
                last = jnp.where(here, turn(high, 2 * i + 2), last)
                put(i, c, low, high)
            yield c, first, last

    local[0].wait()

    def put_adjoint(i, c, low, high):
        a_rows[i + 2, c : c + CB, :128] = low.astype(BF16)
        a_rows[i + 2, c : c + CB, 128:] = high.astype(BF16)

    for c, first, last in split_rows(a_nat, put_adjoint):
        halo_cols[0, c : c + CB, :] = first
        halo_cols[1, c : c + CB, :] = last
    for side in range(2):
        e_own[side] = halo_cols[side].T[: 2 * ROWS, :].astype(BF16)

    local[2].wait()
    local[3].wait()
    local[7].wait()
    obs_row = iota((K, PTS), 0)
    for s in range(2 * N_LON):
        w_own[s // 2, :, PTS * (s % 2) : PTS * (s % 2 + 1)] = jnp.where(
            obs_row < counts[s], w_nat[s].astype(F32), 0.0
        ).astype(BF16)
    for s in range(N_LON):
        p_own[s] = p_nat[2 * s : 2 * s + 2, :]
    w_buf[lon] = w_own[lon]
    p_buf[lon] = p_own[lon]

    local[1].wait()

    def put_input(i, c, low, high):
        at = slice(c, c + CB)
        low_back, high_back = turn(low, 2), turn(high, 2)
        low_on, high_on = turn(low, -2), turn(high, -2)
        x_rows[0, i, at, :128] = jnp.where(lane < 2, 0.0, low_back).astype(BF16)
        x_rows[0, i, at, 128:] = jnp.where(lane < 2, low_back, high_back).astype(BF16)
        x_rows[1, i, at, :128] = low.astype(BF16)
        x_rows[1, i, at, 128:] = high.astype(BF16)
        x_rows[2, i, at, :128] = jnp.where(lane < 126, low_on, high_on).astype(BF16)
        x_rows[2, i, at, 128:] = jnp.where(lane < 126, high_on, 0.0).astype(BF16)

    for c, first, last in split_rows(x_nat, put_input):
        x_edge[0, c : c + CB, :] = last.astype(BF16)
        x_edge[1, c : c + CB, :] = turn(first, 64).astype(BF16)

    groups = CH // GROUP

    def meeting(g, rows):
        at = slice(GROUP * g, GROUP * (g + 1))
        moved = [
            jnp.concatenate([x_rows[b, i, at, :] for b in range(3)], axis=0) for i in rows
        ]
        meets = [
            jnp.concatenate([a_rows[i + 4 - 2 * a, at, :] for a in (0, 1, 2, 2)], axis=0)
            for i in rows
        ]
        return moved, meets

    def pair_up(moved, meets):
        return lax.dot_general(
            jnp.concatenate(moved, axis=1),
            jnp.concatenate(meets, axis=1),
            NT,
            preferred_element_type=F32,
        )

    for g in range(groups):
        g_acc[g] = pair_up(*meeting(g, range(2, ROWS - 2)))

    local[4].wait()
    spread = (iota((GROUP, CH), 1) % GROUP == iota((GROUP, CH), 0)).astype(F32).astype(BF16)
    same_group = iota((CH, CH), 0) // GROUP == iota((CH, CH), 1) // GROUP
    for tap in range(9):
        stacked = jnp.concatenate([w_in[g, tap] for g in range(groups)], axis=0)
        tiled = jnp.dot(stacked, spread, preferred_element_type=F32)
        w_diag[:, CH * tap : CH * (tap + 1)] = jnp.where(same_group, tiled, 0.0).astype(BF16)

    pl.semaphore_wait(barrier, 4 + N_LAT - 1 + N_LON - 1)

    def halo(index, src, dst, to_lat, to_lon):
        return pltpu.make_async_remote_copy(
            src_ref=src,
            dst_ref=dst,
            send_sem=halo_send.at[index],
            recv_sem=halo_recv.at[index],
            device_id=(to_lat, to_lon),
            device_id_type=MESH,
        )

    halos = [
        halo(0, e_own.at[1], e_in.at[0], lat, east),
        halo(1, e_own.at[0], e_in.at[1], lat, west),
        halo(2, e_own.at[1], e_in.at[2], south, east),
        halo(3, e_own.at[0], e_in.at[3], south, west),
        halo(4, e_own.at[1], e_in.at[4], north, east),
        halo(5, e_own.at[0], e_in.at[5], north, west),
    ]
    for part_of in range(2):
        at = pl.ds(CH // 2 * part_of, CH // 2)
        for src, dst, to_lat in ((ROWS, 0, south), (2, ROWS + 2, north)):
            halos.append(
                halo(
                    len(halos),
                    a_rows.at[pl.ds(src, 2), at],
                    a_rows.at[pl.ds(dst, 2), at],
                    to_lat,
                    lon,
                )
            )
    for copy in halos:
        copy.start()

    def obs_copies(k):
        peer = lax.rem(lon + k, N_LON)
        return [
            pltpu.make_async_remote_copy(
                src_ref=src.at[peer],
                dst_ref=dst.at[lon],
                send_sem=obs_send.at[index, k],
                recv_sem=obs_recv.at[index, k],
                device_id=(lat, peer),
                device_id_type=MESH,
            )
            for index, (src, dst) in enumerate(
                ((w_own, w_buf), (obs_v, v_buf), (p_own, p_buf))
            )
        ]

    def start_obs(k, carry):
        for copy in obs_copies(k):
            copy.start()
        return carry

    lax.fori_loop(1, N_LON, start_obs, 0)

    for copy in halos[:6]:
        copy.wait_recv()

    wide_lane = iota((CH, 128), 1)
    for side in range(2):
        upper = e_in[2 + side].astype(F32)[2 * ROWS - 4 :, :]
        lower = e_in[4 + side].astype(F32)[:4, :]
        e_wide[0:4, :] = jnp.where(lat > 0, upper, 0.0)
        e_wide[4 : 4 + 2 * ROWS, :] = e_in[side].astype(F32)
        e_wide[4 + 2 * ROWS : 8 + 2 * ROWS, :] = jnp.where(lat < N_LAT - 1, lower, 0.0)
        e_wide[8 + 2 * ROWS :, :] = jnp.zeros((120 - 2 * ROWS, CH), F32)
        halo_cols[side] = e_wide[...].T
    for a in range(3):
        from_east = turn(halo_cols[1], 4 * a - 8)
        from_west = turn(halo_cols[0], 64 + 4 * a - 8)
        a_edge[a] = jnp.where(wide_lane < 64, from_east, from_west).astype(BF16)

    scale = 1.0 / math.sqrt(CELLS * N_LAT * N_LON)
    nothing = jnp.zeros((GROUP, 128), BF16)
    tile_lane = iota((3 * GROUP, 128), 1)
    done = []
    for g in range(groups):
        if g % 4 == 0:
            half = pl.ds(CH // 2 * (g // 4), CH // 2)
            for copy in halos[6 + g // 2 : 8 + g // 2]:
                copy.wait_recv()

            @pl.when(lat == 0)
            def _(half=half):
                a_rows[0:2, half] = jnp.zeros((2, CH // 2, COLS), BF16)

            @pl.when(lat == N_LAT - 1)
            def _(half=half):
                a_rows[ROWS + 2 : ROWS + 4, half] = jnp.zeros((2, CH // 2, COLS), BF16)

        at = slice(GROUP * g, GROUP * (g + 1))
        moved, meets = meeting(g, (0, 1, ROWS - 2, ROWS - 1))
        moved.append(jnp.concatenate([x_edge[0, at, :], nothing, x_edge[1, at, :]], axis=0))
        meets.append(jnp.concatenate([a_edge[a, at, :] for a in (0, 1, 2, 2)], axis=0))
        total = (pair_up(moved, meets) + g_acc[g]) * scale
        done.append(total)
        if g % 2 == 1:
            at = 96 * (g // 2)
            grad[at : at + 96, :] = jnp.where(tile_lane < 64, done[g - 1], turn(total, 64))
        if g % 4 == 3:
            value = turn(done[g - 3], -64)
            for m in range(1, 4):
                shifted = turn(done[g - 3 + m], 32 * m - 64)
                value = jnp.where(tile_lane // GROUP == m, shifted, value)
            at = 384 + 96 * (g // 4)
            grad[at : at + 96, :] = value
    grad[576:640, :] = jnp.zeros((64, 128), F32)

    def rs_copy(k):
        peer = lax.rem(lon + k, N_LON)
        return pltpu.make_async_remote_copy(
            src_ref=grad.at[pl.ds(pl.multiple_of(CHUNK * peer, 8), CHUNK), :],
            dst_ref=rs_buf.at[k],
            send_sem=rs_send.at[k],
            recv_sem=rs_recv.at[k],
            device_id=(lat, peer),
            device_id_type=MESH,
        )

    def start_rs(k, carry):
        rs_copy(k).start()
        return carry

    lax.fori_loop(1, N_LON, start_rs, 0)

    for row in range(ROWS + 4):
        for c in range(0, CH, CB):
            at = slice(c, c + CB)
            low = a_rows[row, at, :128].astype(F32)
            high = a_rows[row, at, 128:].astype(F32)
            low_on, high_on = turn(low, -2), turn(high, -2)
            low_back, high_back = turn(low, 2), turn(high, 2)
            east_cols = turn(halo_cols[1, at, :], 126 - 2 * row)
            west_cols = turn(halo_cols[0, at, :], -2 * row)
            a_shift[0, row, at, :128] = jnp.where(lane < 126, low_on, high_on).astype(BF16)
            a_shift[0, row, at, 128:] = jnp.where(lane < 126, high_on, east_cols).astype(BF16)
            a_shift[1, row, at, :128] = jnp.where(lane < 2, west_cols, low_back).astype(BF16)
            a_shift[1, row, at, 128:] = jnp.where(lane < 2, low_back, high_back).astype(BF16)

    for copy in (local[5], local[6], local[8]):
        copy.wait()

    def wait_obs(k, carry):
        for copy in obs_copies(k):
            copy.wait_recv()
        return carry

    lax.fori_loop(1, N_LON, wait_obs, 0)
    owners = [owner[t] for t in range(TRACKS)]
    places = [
        jnp.minimum(
            sum([(owners[u] == owners[t]).astype(jnp.int32) for u in range(t)], jnp.int32(0)), 1
        )
        for t in range(TRACKS)
    ]
    cells = fp[...]
    width = COLS * N_LON
    rows_of = (cells // width - lat * ROWS).astype(F32).astype(BF16)
    cols_of = (cells % width - lon * COLS).astype(F32).astype(BF16)
    widen = (iota((PTS, 4 * PTS), 1) % PTS == iota((PTS, 4 * PTS), 0)).astype(F32).astype(BF16)
    cell = COLS * jnp.dot(rows_of, widen, preferred_element_type=F32) + jnp.dot(
        cols_of, widen, preferred_element_type=F32
    )
    widen_pair = jnp.concatenate([widen, widen], axis=0)
    slot_lane = iota((K, 2 * PTS), 1) // PTS
    own_lanes = iota((TRACKS, 4 * PTS), 1) // PTS == iota((TRACKS, 4 * PTS), 0) % 4
    cell = jnp.where(own_lanes, cell, 0.0)
    same_track = iota((4 * K, 4 * PTS), 0) // K == iota((4 * K, 4 * PTS), 1) // PTS
    for q in range(4):
        tracks = range(4 * q, 4 * q + 4)
        stacked = jnp.concatenate(
            [jnp.where(slot_lane == places[t], w_buf[owners[t]].astype(F32), 0.0) for t in tracks],
            axis=0,
        )
        tiled = jnp.dot(stacked.astype(BF16), widen_pair, preferred_element_type=F32)
        blocks[q] = jnp.where(same_track, tiled, 0.0).astype(BF16)
        cell_row[q : q + 1, :] = jnp.sum(cell[4 * q : 4 * q + 4, :], axis=0, keepdims=True)

    def build_op(i, carry):
        here = (iota((COLS, 4 * PTS), 0) + i * COLS).astype(F32)
        at = pl.ds(pl.multiple_of(i * COLS, COLS), COLS)
        for q in range(4):
            hit = jnp.where(here == cell_row[q : q + 1, :], 1.0, 0.0).astype(BF16)
            obs_op[at, 4 * K * q : 4 * K * (q + 1)] = lax.dot_general(
                hit, blocks[q], NT, preferred_element_type=F32
            ).astype(BF16)
        return carry

    lax.fori_loop(0, ROWS, build_op, 0)

    def wait_rs(k, carry):
        rs_copy(k).wait_recv()
        return carry

    lax.fori_loop(1, N_LON, wait_rs, 0)
    own = grad[pl.ds(pl.multiple_of(CHUNK * lon, 8), CHUNK), :]
    for k in range(1, N_LON):
        own += rs_buf[k]
    part[...] = own
    ex_buf[lat] = own

    def ex_copy(k):
        return pltpu.make_async_remote_copy(
            src_ref=part,
            dst_ref=ex_buf.at[lat],
            send_sem=ex_send.at[k],
            recv_sem=ex_recv.at[k],
            device_id=(lax.rem(lat + k, N_LAT), lon),
            device_id_type=MESH,
        )

    for k in range(1, N_LAT):
        ex_copy(k).start()

    model_obs = jnp.dot(
        jnp.concatenate([x_rows[1, i] for i in range(ROWS)], axis=1),
        obs_op[...],
        preferred_element_type=F32,
    ).T

    def p_row(which, place):
        pair = p_buf[which].astype(F32)
        return jnp.where(place == 0, pair[0:1, :], pair[1:2, :])

    pieces = []
    for t in range(TRACKS):
        value = v_buf[owners[t], places[t]].astype(F32)
        precision = p_row(owners[t], places[t])
        pieces.append((model_obs[K * t : K * (t + 1), :] - value) * precision)
    misfit_t = jnp.concatenate(pieces, axis=0).T.astype(BF16)

    def finish_rows(first, last):
        def one(i, carry):
            fields = []
            for a in range(3):
                row = i + 4 - 2 * a
                fields += [a_shift[0, row], a_rows[row], a_shift[1, row]]
            total = a_rows[i + 2].astype(F32) + jnp.dot(
                w_diag[...], jnp.concatenate(fields, axis=0), preferred_element_type=F32
            )
            at = pl.ds(pl.multiple_of(i * COLS, COLS), COLS)
            total += lax.dot_general(misfit_t, obs_op[at, :], NT, preferred_element_type=F32)
            for half in range(2):
                f_buf[half, pl.ds(i, CH, stride=ROWS), :] = total[
                    :, 128 * half : 128 * half + 128
                ]
            return carry

        lax.fori_loop(first, last, one, 0)

    for k in range(1, N_LAT):
        ex_copy(k).wait_recv()
    whole = ex_buf[0]
    for k in range(1, N_LAT):
        whole += ex_buf[k]
    mine = pl.ds(pl.multiple_of(CHUNK * lon, 8), CHUNK)
    gathered[mine, :] = whole

    def ag_copy(k):
        return pltpu.make_async_remote_copy(
            src_ref=gathered.at[mine, :],
            dst_ref=gathered.at[mine, :],
            send_sem=ag_send.at[k],
            recv_sem=ag_recv.at[k],
            device_id=(lat, lax.rem(lon + k, N_LON)),
            device_id_type=MESH,
        )

    def start_ag(k, carry):
        ag_copy(k).start()
        return carry

    lax.fori_loop(1, N_LON, start_ag, 0)
    finish_rows(0, ROWS)
    for half in range(2):
        out[:, :, 128 * half : 128 * half + 128] = (
            f_buf[half].reshape(CH, ROWS, 128).astype(BF16)
        )

    def wait_ag(k, carry):
        ag_copy(k).wait_recv()
        return carry

    lax.fori_loop(1, N_LON, wait_ag, 0)
    for g in range(groups):
        for a in range(3):
            if a < 2:
                at, shift = 96 * (g // 2), 64 * (g % 2) + GROUP * a
            else:
                at, shift = 384 + 96 * (g // 4), GROUP * (g % 4)
            value = turn(gathered[at : at + 96, :], -shift)[:, :GROUP]
            for b in range(3):
                grad_out[g, 3 * a + b] = value[GROUP * b : GROUP * (b + 1), :]

    for copy in halos:
        copy.wait_send()

    def wait_sends(k, carry):
        for copy in obs_copies(k):
            copy.wait_send()
        rs_copy(k).wait_send()
        ag_copy(k).wait_send()
        return carry

    lax.fori_loop(1, N_LON, wait_sends, 0)
    for k in range(1, N_LAT):
        ex_copy(k).wait_send()


def on_device(
    adjoint_in,
    layer_input,
    conv_weight,
    footprint,
    owner,
    obs_weight,
    obs_value,
    obs_precision,
    obs_count,
):
    anywhere = pl.BlockSpec(memory_space=pltpu.HBM)
    vmem = pl.BlockSpec(memory_space=pltpu.VMEM)
    return pl.pallas_call(
        kernel,
        out_shape=(
            jax.ShapeDtypeStruct((CH, ROWS, COLS), BF16),
            jax.ShapeDtypeStruct((CH // GROUP, 9, GROUP, GROUP), F32),
        ),
        in_specs=[anywhere] * 9,
        out_specs=(vmem, vmem),
        scratch_shapes=[
            pltpu.SMEM((TRACKS,), jnp.int32),
            pltpu.SMEM((2 * N_LON,), jnp.int32),
            pltpu.VMEM((TRACKS, PTS), jnp.int32),
            pltpu.VMEM((CH, ROWS, COLS), BF16),
            pltpu.VMEM((CH, ROWS, COLS), BF16),
            pltpu.VMEM((2, CELLS, 128), F32),
            pltpu.VMEM((ROWS + 4, CH, COLS), BF16),
            pltpu.VMEM((2, ROWS + 4, CH, COLS), BF16),
            pltpu.VMEM((3, ROWS, CH, COLS), BF16),
            pltpu.VMEM((2, CH, 128), BF16),
            pltpu.VMEM((2, 2 * ROWS, CH), BF16),
            pltpu.VMEM((6, 2 * ROWS, CH), BF16),
            pltpu.VMEM((128, CH), F32),
            pltpu.VMEM((2, CH, 128), F32),
            pltpu.VMEM((3, CH, 128), BF16),
            pltpu.VMEM((CH // GROUP, 9, GROUP, GROUP), BF16),
            pltpu.VMEM((CH, 9 * CH), BF16),
            pltpu.VMEM((CELLS, TRACKS * K), BF16),
            pltpu.VMEM((4, 4 * K, 4 * PTS), BF16),
            pltpu.VMEM((8, 4 * PTS), F32),
            pltpu.VMEM((2 * N_LON, K, PTS), BF16),
            pltpu.VMEM((2 * N_LON, CH), BF16),
            pltpu.VMEM((N_LON, K, 2 * PTS), BF16),
            pltpu.VMEM((N_LON, 2, CH), BF16),
            pltpu.VMEM((N_LON, K, 2 * PTS), BF16),
            pltpu.VMEM((N_LON, 2, K, CH), BF16),
            pltpu.VMEM((N_LON, 2, CH), BF16),
            pltpu.VMEM((640, 128), F32),
            pltpu.VMEM((CH // GROUP, 96, 128), F32),
            pltpu.VMEM((N_LON, CHUNK, 128), F32),
            pltpu.VMEM((CHUNK, 128), F32),
            pltpu.VMEM((N_LAT, CHUNK, 128), F32),
            pltpu.VMEM((640, 128), F32),
            pltpu.SemaphoreType.DMA((9,)),
            pltpu.SemaphoreType.DMA((10,)),
            pltpu.SemaphoreType.DMA((10,)),
            pltpu.SemaphoreType.DMA((3, N_LON)),
            pltpu.SemaphoreType.DMA((3, N_LON)),
            pltpu.SemaphoreType.DMA((N_LON,)),
            pltpu.SemaphoreType.DMA((N_LON,)),
            pltpu.SemaphoreType.DMA((N_LAT,)),
            pltpu.SemaphoreType.DMA((N_LAT,)),
            pltpu.SemaphoreType.DMA((N_LON,)),
            pltpu.SemaphoreType.DMA((N_LON,)),
        ],
        compiler_params=pltpu.CompilerParams(
            collective_id=0, has_side_effects=True, vmem_limit_bytes=44 * 1024 * 1024
        ),
    )(
        *(
            pltpu.with_memory_space_constraint(value, pltpu.HBM)
            for value in (
                owner.reshape(TRACKS),
                obs_count,
                footprint,
                adjoint_in,
                layer_input,
                conv_weight,
                obs_weight,
                obs_value.reshape(N_LON, 2, K, CH),
                obs_precision,
            )
        ),
    )


def solution(mesh):
    in_specs = (
        P(None, "lat", "lon"),
        P(None, "lat", "lon"),
        P(),
        P(("lat", "lon"), None),
        P(("lat", "lon"), None),
        P(("lat", "lon"), None, None),
        P(("lat", "lon"), None, None),
        P(("lat", "lon"), None),
        P(("lat", "lon")),
    )
    out_specs = (P(None, "lat", "lon"), P())
    return jax.shard_map(
        on_device, mesh=mesh, in_specs=in_specs, out_specs=out_specs, check_vma=False
    )
```

```python
import math

import jax
import jax.numpy as jnp
from jax import lax
from jax.experimental import pallas as pl
from jax.experimental.pallas import tpu as pltpu
from jax.sharding import PartitionSpec as P

MESH = pl.DeviceIdType.MESH
N_LAT = 8
N_LON = 16
CH = 256
ROWS = 8
COLS = 256
CELLS = ROWS * COLS
GROUP = 32
TRACKS = 16
K = 32
PTS = 64
CHUNK = 5
CB = 64
F32 = jnp.float32
BF16 = jnp.bfloat16
NT = (((1,), (1,)), ((), ()))
STEPS = sorted(
    ((a, b) for a in range(4) for b in range(4) if a or b),
    key=lambda step: -min(step[0], 4 - step[0]) - min(step[1], 4 - step[1]),
)
PACK = 96


def iota(shape, dim):
    return lax.broadcasted_iota(jnp.int32, shape, dim)


def turn(value, shift):
    return pltpu.roll(value, shift % 128, 1) if shift % 128 else value


def kernel(
    owner_in,
    counts_in,
    fp_in,
    adj_in,
    x_in,
    conv_w,
    obs_w,
    obs_v,
    obs_p,
    out,
    grad_out,
    owner,
    counts,
    fp,
    a_nat,
    x_nat,
    f_buf,
    a_rows,
    a_shift,
    x_rows,
    x_edge,
    e_own,
    e_in,
    e_wide,
    halo_cols,
    a_edge,
    w_in,
    w_diag,
    total,
    obs_op,
    blocks,
    cell_row,
    w_nat,
    p_nat,
    packed,
    early,
    late,
    grad,
    g_acc,
    rs_buf,
    part,
    ex_buf,
    gathered,
    local_sem,
    halo_send,
    halo_recv,
    obs_send,
    obs_recv,
    rs_send,
    rs_recv,
    ex_send,
    ex_recv,
    ag_send,
    ag_recv,
):
    lat = lax.axis_index("lat")
    lon = lax.axis_index("lon")
    north = lax.rem(lat + N_LAT - 1, N_LAT)
    south = lax.rem(lat + 1, N_LAT)
    west = lax.rem(lon + N_LON - 1, N_LON)
    east = lax.rem(lon + 1, N_LON)
    outer, inner = lon // 4, lax.rem(lon, 4)
    peers = [4 * lax.rem(outer + a, 4) + lax.rem(inner + b, 4) for a, b in STEPS]

    local = [
        pltpu.make_async_copy(src, dst, local_sem.at[index])
        for index, (src, dst) in enumerate(
            (
                (adj_in, a_nat),
                (x_in, x_nat),
                (obs_w, w_nat),
                (obs_p, p_nat),
                (conv_w, w_in),
                (obs_v.at[:, 0], packed.at[:, pl.ds(0, K), :]),
                (obs_v.at[:, 1], packed.at[:, pl.ds(2 * K, K), :]),
                (owner_in, owner),
                (counts_in, counts),
                (fp_in, fp),
            )
        )
    ]
    for copy in local:
        copy.start()

    barrier = pltpu.get_barrier_semaphore()

    def greet(to_lat, to_lon):
        pl.semaphore_signal(barrier, inc=1, device_id=(to_lat, to_lon), device_id_type=MESH)

    for to_lat, to_lon in ((north, west), (north, east), (south, west), (south, east)):
        greet(to_lat, to_lon)
    for k in range(1, N_LAT):
        greet(lax.rem(lat + k, N_LAT), lon)
    for peer in peers:
        greet(lat, peer)

    lane = iota((CB, 128), 1)

    def split_rows(native, put):
        for half in range(2):
            f_buf[half] = (
                native[:, :, 128 * half : 128 * half + 128].astype(F32).reshape(CELLS, 128)
            )
        for c in range(0, CH, CB):
            first = jnp.zeros((CB, 128), F32)
            last = jnp.zeros((CB, 128), F32)
            for i in range(ROWS):
                low = f_buf[0, pl.ds(ROWS * c + i, CB, stride=ROWS), :]
                high = f_buf[1, pl.ds(ROWS * c + i, CB, stride=ROWS), :]
                here = lane // 2 == i
                first = jnp.where(here, turn(low, 2 * i), first)
                last = jnp.where(here, turn(high, 2 * i + 2), last)
                put(i, c, low, high)
            yield c, first, last

    local[0].wait()

    def put_adjoint(i, c, low, high):
        a_rows[i + 2, c : c + CB, :128] = low.astype(BF16)
        a_rows[i + 2, c : c + CB, 128:] = high.astype(BF16)

    for c, first, last in split_rows(a_nat, put_adjoint):
        halo_cols[0, c : c + CB, :] = first
        halo_cols[1, c : c + CB, :] = last
    for side in range(2):
        e_own[side] = halo_cols[side].T[: 2 * ROWS, :].astype(BF16)

    local[2].wait()
    local[3].wait()
    local[8].wait()
    obs_row = iota((K, PTS), 0)
    for s in range(2 * N_LON):
        packed[s // 2, K : 2 * K, PTS * (s % 2) : PTS * (s % 2 + 1)] = jnp.where(
            obs_row < counts[s], w_nat[s].astype(F32), 0.0
        ).astype(BF16)
        for half in range(2):
            at = K + 2 * (s % 2) + half
            packed[s // 2, at : at + 1, 128:] = p_nat[
                s : s + 1, 128 * half : 128 * half + 128
            ]
    local[5].wait()
    local[6].wait()
    early[lon] = packed[lon, : 2 * K]
    late[lon] = packed[lon, 2 * K :]

    local[1].wait()

    def put_input(i, c, low, high):
        at = slice(c, c + CB)
        low_back, high_back = turn(low, 2), turn(high, 2)
        low_on, high_on = turn(low, -2), turn(high, -2)
        x_rows[0, i, at, :128] = jnp.where(lane < 2, 0.0, low_back).astype(BF16)
        x_rows[0, i, at, 128:] = jnp.where(lane < 2, low_back, high_back).astype(BF16)
        x_rows[1, i, at, :128] = low.astype(BF16)
        x_rows[1, i, at, 128:] = high.astype(BF16)
        x_rows[2, i, at, :128] = jnp.where(lane < 126, low_on, high_on).astype(BF16)
        x_rows[2, i, at, 128:] = jnp.where(lane < 126, high_on, 0.0).astype(BF16)

    for c, first, last in split_rows(x_nat, put_input):
        x_edge[0, c : c + CB, :] = last.astype(BF16)
        x_edge[1, c : c + CB, :] = turn(first, 64).astype(BF16)

    groups = CH // GROUP

    def meeting(g, rows):
        at = slice(GROUP * g, GROUP * (g + 1))
        moved = [
            jnp.concatenate([x_rows[b, i, at, :] for b in range(3)], axis=0) for i in rows
        ]
        meets = [
            jnp.concatenate([a_rows[i + 4 - 2 * a, at, :] for a in (0, 1, 2, 2)], axis=0)
            for i in rows
        ]
        return moved, meets

    def pair_up(moved, meets):
        return lax.dot_general(
            jnp.concatenate(moved, axis=1),
            jnp.concatenate(meets, axis=1),
            NT,
            preferred_element_type=F32,
        )

    for g in range(groups):
        g_acc[g] = pair_up(*meeting(g, range(2, ROWS - 2)))

    local[4].wait()
    spread = (iota((GROUP, CH), 1) % GROUP == iota((GROUP, CH), 0)).astype(F32).astype(BF16)
    same_group = iota((CH, CH), 0) // GROUP == iota((CH, CH), 1) // GROUP
    for tap in range(9):
        stacked = jnp.concatenate([w_in[g, tap] for g in range(groups)], axis=0)
        tiled = jnp.dot(stacked, spread, preferred_element_type=F32)
        w_diag[:, CH * tap : CH * (tap + 1)] = jnp.where(same_group, tiled, 0.0).astype(BF16)

    def weigh(taps, fields):
        weights = [w_diag[:, CH * tap : CH * (tap + 1)] for tap in taps]
        return jnp.dot(
            jnp.concatenate(weights, axis=1),
            jnp.concatenate(fields, axis=0),
            preferred_element_type=F32,
        )

    def rows_of_taps(i):
        return [(a, i + 4 - 2 * a, 2 <= i + 4 - 2 * a < ROWS + 2) for a in range(3)]

    for i in range(ROWS):
        here = [(a, row) for a, row, own_row in rows_of_taps(i) if own_row]
        total[i] = a_rows[i + 2].astype(F32) + weigh(
            [3 * a + 1 for a, _ in here], [a_rows[row] for _, row in here]
        )

    pl.semaphore_wait(barrier, 4 + N_LAT - 1 + N_LON - 1)

    def halo(index, src, dst, to_lat, to_lon):
        return pltpu.make_async_remote_copy(
            src_ref=src,
            dst_ref=dst,
            send_sem=halo_send.at[index],
            recv_sem=halo_recv.at[index],
            device_id=(to_lat, to_lon),
            device_id_type=MESH,
        )

    halos = [
        halo(0, e_own.at[1], e_in.at[0], lat, east),
        halo(1, e_own.at[0], e_in.at[1], lat, west),
        halo(2, e_own.at[1], e_in.at[2], south, east),
        halo(3, e_own.at[0], e_in.at[3], south, west),
        halo(4, e_own.at[1], e_in.at[4], north, east),
        halo(5, e_own.at[0], e_in.at[5], north, west),
    ]
    for part_of in range(2):
        at = pl.ds(CH // 2 * part_of, CH // 2)
        for src, dst, to_lat in ((ROWS, 0, south), (2, ROWS + 2, north)):
            halos.append(
                halo(
                    len(halos),
                    a_rows.at[pl.ds(src, 2), at],
                    a_rows.at[pl.ds(dst, 2), at],
                    to_lat,
                    lon,
                )
            )
    for copy in halos:
        copy.start()

    def obs_copy(k, which):
        at = (pl.ds(0, 2 * K), pl.ds(2 * K, K))[which]
        return pltpu.make_async_remote_copy(
            src_ref=packed.at[peers[k], at],
            dst_ref=(early, late)[which].at[lon],
            send_sem=obs_send.at[which, k],
            recv_sem=obs_recv.at[which, k],
            device_id=(lat, peers[k]),
            device_id_type=MESH,
        )

    for k in range(N_LON - 1):
        obs_copy(k, 0).start()

    for copy in halos[:6]:
        copy.wait_recv()

    wide_lane = iota((CH, 128), 1)
    for side in range(2):
        upper = e_in[2 + side].astype(F32)[2 * ROWS - 4 :, :]
        lower = e_in[4 + side].astype(F32)[:4, :]
        e_wide[0:4, :] = jnp.where(lat > 0, upper, 0.0)
        e_wide[4 : 4 + 2 * ROWS, :] = e_in[side].astype(F32)
        e_wide[4 + 2 * ROWS : 8 + 2 * ROWS, :] = jnp.where(lat < N_LAT - 1, lower, 0.0)
        e_wide[8 + 2 * ROWS :, :] = jnp.zeros((120 - 2 * ROWS, CH), F32)
        halo_cols[side] = e_wide[...].T
    for a in range(3):
        from_east = turn(halo_cols[1], 4 * a - 8)
        from_west = turn(halo_cols[0], 64 + 4 * a - 8)
        a_edge[a] = jnp.where(wide_lane < 64, from_east, from_west).astype(BF16)

    scale = 1.0 / math.sqrt(CELLS * N_LAT * N_LON)
    nothing = jnp.zeros((GROUP, 128), BF16)
    tile_lane = iota((3 * GROUP, 128), 1)
    done = []

    def put_grad(at, value):
        grad[at : at + 12] = value.reshape(12, 8, 128).astype(BF16)

    for g in range(groups):
        if g % 4 == 0:
            half = pl.ds(CH // 2 * (g // 4), CH // 2)
            for copy in halos[6 + g // 2 : 8 + g // 2]:
                copy.wait_recv()

            @pl.when(lat == 0)
            def _(half=half):
                a_rows[0:2, half] = jnp.zeros((2, CH // 2, COLS), BF16)

            @pl.when(lat == N_LAT - 1)
            def _(half=half):
                a_rows[ROWS + 2 : ROWS + 4, half] = jnp.zeros((2, CH // 2, COLS), BF16)

        at = slice(GROUP * g, GROUP * (g + 1))
        moved, meets = meeting(g, (0, 1, ROWS - 2, ROWS - 1))
        moved.append(jnp.concatenate([x_edge[0, at, :], nothing, x_edge[1, at, :]], axis=0))
        meets.append(jnp.concatenate([a_edge[a, at, :] for a in (0, 1, 2, 2)], axis=0))
        value = (pair_up(moved, meets) + g_acc[g]) * scale
        done.append(value)
        if g % 2 == 1:
            put_grad(12 * (g // 2), jnp.where(tile_lane < 64, done[g - 1], turn(value, 64)))
        if g % 4 == 3:
            value = turn(done[g - 3], -64)
            for m in range(1, 4):
                shifted = turn(done[g - 3 + m], 32 * m - 64)
                value = jnp.where(tile_lane // GROUP == m, shifted, value)
            put_grad(48 + 12 * (g // 4), value)
    grad[72:] = jnp.zeros((8, 8, 128), BF16)

    def rs_copy(k):
        return pltpu.make_async_remote_copy(
            src_ref=grad.at[pl.ds(CHUNK * peers[k], CHUNK)],
            dst_ref=rs_buf.at[k],
            send_sem=rs_send.at[k],
            recv_sem=rs_recv.at[k],
            device_id=(lat, peers[k]),
            device_id_type=MESH,
        )

    for k in range(N_LON - 1):
        rs_copy(k).start()
    for k in range(N_LON - 1):
        obs_copy(k, 1).start()

    for row in range(ROWS + 4):
        for c in range(0, CH, CB):
            at = slice(c, c + CB)
            low = a_rows[row, at, :128].astype(F32)
            high = a_rows[row, at, 128:].astype(F32)
            low_on, high_on = turn(low, -2), turn(high, -2)
            low_back, high_back = turn(low, 2), turn(high, 2)
            east_cols = turn(halo_cols[1, at, :], 126 - 2 * row)
            west_cols = turn(halo_cols[0, at, :], -2 * row)
            a_shift[0, row, at, :128] = jnp.where(lane < 126, low_on, high_on).astype(BF16)
            a_shift[0, row, at, 128:] = jnp.where(lane < 126, high_on, east_cols).astype(BF16)
            a_shift[1, row, at, :128] = jnp.where(lane < 2, west_cols, low_back).astype(BF16)
            a_shift[1, row, at, 128:] = jnp.where(lane < 2, low_back, high_back).astype(BF16)

    for copy in (local[7], local[9]):
        copy.wait()
    for k in range(N_LON - 1):
        obs_copy(k, 0).wait_recv()
    owners = [owner[t] for t in range(TRACKS)]
    places = [
        jnp.minimum(
            sum([(owners[u] == owners[t]).astype(jnp.int32) for u in range(t)], jnp.int32(0)), 1
        )
        for t in range(TRACKS)
    ]
    cells = fp[...]
    width = COLS * N_LON
    rows_of = (cells // width - lat * ROWS).astype(F32).astype(BF16)
    cols_of = (cells % width - lon * COLS).astype(F32).astype(BF16)
    widen = (iota((PTS, 4 * PTS), 1) % PTS == iota((PTS, 4 * PTS), 0)).astype(F32).astype(BF16)
    cell = COLS * jnp.dot(rows_of, widen, preferred_element_type=F32) + jnp.dot(
        cols_of, widen, preferred_element_type=F32
    )
    widen_pair = jnp.concatenate([widen, widen], axis=0)
    slot_lane = iota((K, 2 * PTS), 1) // PTS
    own_lanes = iota((TRACKS, 4 * PTS), 1) // PTS == iota((TRACKS, 4 * PTS), 0) % 4
    cell = jnp.where(own_lanes, cell, 0.0)
    same_track = iota((4 * K, 4 * PTS), 0) // K == iota((4 * K, 4 * PTS), 1) // PTS
    for q in range(4):
        tracks = range(4 * q, 4 * q + 4)
        stacked = jnp.concatenate(
            [jnp.where(slot_lane == places[t], early[owners[t], K : 2 * K, :128].astype(F32), 0.0) for t in tracks],
            axis=0,
        )
        tiled = jnp.dot(stacked.astype(BF16), widen_pair, preferred_element_type=F32)
        blocks[q] = jnp.where(same_track, tiled, 0.0).astype(BF16)
        cell_row[q : q + 1, :] = jnp.sum(cell[4 * q : 4 * q + 4, :], axis=0, keepdims=True)

    def build_op(i, carry):
        here = (iota((COLS, 4 * PTS), 0) + i * COLS).astype(F32)
        at = pl.ds(pl.multiple_of(i * COLS, COLS), COLS)
        for q in range(4):
            hit = jnp.where(here == cell_row[q : q + 1, :], 1.0, 0.0).astype(BF16)
            obs_op[at, 4 * K * q : 4 * K * (q + 1)] = lax.dot_general(
                hit, blocks[q], NT, preferred_element_type=F32
            ).astype(BF16)
        return carry

    lax.fori_loop(0, ROWS, build_op, 0)

    own = grad[pl.ds(CHUNK * lon, CHUNK)].astype(F32)
    for k in range(N_LON - 1):
        rs_copy(k).wait_recv()
        own += rs_buf[k].astype(F32)
    part[...] = own
    ex_buf[lat] = own

    def ex_copy(k):
        return pltpu.make_async_remote_copy(
            src_ref=part,
            dst_ref=ex_buf.at[lat],
            send_sem=ex_send.at[k],
            recv_sem=ex_recv.at[k],
            device_id=(lax.rem(lat + k, N_LAT), lon),
            device_id_type=MESH,
        )

    for k in range(1, N_LAT):
        ex_copy(k).start()

    model_obs = jnp.dot(
        jnp.concatenate([x_rows[1, i] for i in range(ROWS)], axis=1),
        obs_op[...],
        preferred_element_type=F32,
    ).T

    def p_row(which, place):
        rows = early[which, K : K + 4, 128:].astype(F32)
        first = jnp.concatenate([rows[0:1, :], rows[1:2, :]], axis=1)
        second = jnp.concatenate([rows[2:3, :], rows[3:4, :]], axis=1)
        return jnp.where(place == 0, first, second)

    pieces = []
    for k in range(N_LON - 1):
        obs_copy(k, 1).wait_recv()
    for t in range(TRACKS):
        value = jnp.where(
            places[t] == 0,
            early[owners[t], :K, :].astype(F32),
            late[owners[t]].astype(F32),
        )
        precision = p_row(owners[t], places[t])
        pieces.append((model_obs[K * t : K * (t + 1), :] - value) * precision)
    misfit_t = jnp.concatenate(pieces, axis=0).T.astype(BF16)

    def finish_row(i):
        taps, fields = [], []
        for a, row, own_row in rows_of_taps(i):
            taps += [3 * a, 3 * a + 2]
            fields += [a_shift[0, row], a_shift[1, row]]
            if not own_row:
                taps.append(3 * a + 1)
                fields.append(a_rows[row])
        done_row = (
            total[i]
            + weigh(taps, fields)
            + lax.dot_general(
                misfit_t,
                obs_op[COLS * i : COLS * (i + 1), :],
                NT,
                preferred_element_type=F32,
            )
        )
        for half in range(2):
            f_buf[half, pl.ds(i, CH, stride=ROWS), :] = done_row[:, 128 * half : 128 * half + 128]

    for k in range(1, N_LAT):
        ex_copy(k).wait_recv()
    whole = ex_buf[0]
    for k in range(1, N_LAT):
        whole += ex_buf[k]
    mine = pl.ds(CHUNK * lon, CHUNK)
    gathered[mine] = whole.astype(BF16)

    def ag_copy(k):
        return pltpu.make_async_remote_copy(
            src_ref=gathered.at[mine],
            dst_ref=gathered.at[mine],
            send_sem=ag_send.at[k],
            recv_sem=ag_recv.at[k],
            device_id=(lat, peers[k]),
            device_id_type=MESH,
        )

    for k in range(N_LON - 1):
        ag_copy(k).start()
    for i in range(ROWS):
        finish_row(i)
    for half in range(2):
        out[:, :, 128 * half : 128 * half + 128] = (
            f_buf[half].reshape(CH, ROWS, 128).astype(BF16)
        )

    for copy in halos:
        copy.wait_send()
    for k in range(1, N_LAT):
        ex_copy(k).wait_send()
    for k in range(N_LON - 1):
        obs_copy(k, 0).wait_send()
        obs_copy(k, 1).wait_send()
        rs_copy(k).wait_send()
        ag_copy(k).wait_send()
    for k in range(N_LON - 1):
        ag_copy(k).wait_recv()
    grad_out[...] = gathered[...]


def unpack(field, grad, out, grad_out, blocks, sem):
    copy = pltpu.make_async_copy(field, out, sem.at[0])
    copy.start()
    for g in range(CH // GROUP):
        for a in range(3):
            if a < 2:
                at, shift = 12 * (g // 2), 64 * (g % 2) + GROUP * a
            else:
                at, shift = 48 + 12 * (g // 4), GROUP * (g % 4)
            value = turn(grad[at : at + 12].astype(F32).reshape(96, 128), -shift)[:, :GROUP]
            for b in range(3):
                blocks[g, 3 * a + b] = value[GROUP * b : GROUP * (b + 1), :]
    copy_grad = pltpu.make_async_copy(blocks, grad_out, sem.at[1])
    copy_grad.start()
    copy.wait()
    copy_grad.wait()


def on_device(
    adjoint_in,
    layer_input,
    conv_weight,
    footprint,
    owner,
    obs_weight,
    obs_value,
    obs_precision,
    obs_count,
):
    anywhere = pl.BlockSpec(memory_space=pltpu.HBM)
    vmem = pl.BlockSpec(memory_space=pltpu.VMEM)
    field, grad = pl.pallas_call(
        kernel,
        out_shape=(
            jax.ShapeDtypeStruct((CH, ROWS, COLS), BF16),
            jax.ShapeDtypeStruct((N_LON * CHUNK, 8, 128), BF16),
        ),
        in_specs=[anywhere] * 9,
        out_specs=(vmem, vmem),
        scratch_shapes=[
            pltpu.SMEM((TRACKS,), jnp.int32),
            pltpu.SMEM((2 * N_LON,), jnp.int32),
            pltpu.VMEM((TRACKS, PTS), jnp.int32),
            pltpu.VMEM((CH, ROWS, COLS), BF16),
            pltpu.VMEM((CH, ROWS, COLS), BF16),
            pltpu.VMEM((2, CELLS, 128), F32),
            pltpu.VMEM((ROWS + 4, CH, COLS), BF16),
            pltpu.VMEM((2, ROWS + 4, CH, COLS), BF16),
            pltpu.VMEM((3, ROWS, CH, COLS), BF16),
            pltpu.VMEM((2, CH, 128), BF16),
            pltpu.VMEM((2, 2 * ROWS, CH), BF16),
            pltpu.VMEM((6, 2 * ROWS, CH), BF16),
            pltpu.VMEM((128, CH), F32),
            pltpu.VMEM((2, CH, 128), F32),
            pltpu.VMEM((3, CH, 128), BF16),
            pltpu.VMEM((CH // GROUP, 9, GROUP, GROUP), BF16),
            pltpu.VMEM((CH, 9 * CH), BF16),
            pltpu.VMEM((ROWS, CH, COLS), F32),
            pltpu.VMEM((CELLS, TRACKS * K), BF16),
            pltpu.VMEM((4, 4 * K, 4 * PTS), BF16),
            pltpu.VMEM((8, 4 * PTS), F32),
            pltpu.VMEM((2 * N_LON, K, PTS), BF16),
            pltpu.VMEM((2 * N_LON, CH), BF16),
            pltpu.VMEM((N_LON, PACK, CH), BF16),
            pltpu.VMEM((N_LON, 2 * K, CH), BF16),
            pltpu.VMEM((N_LON, K, CH), BF16),
            pltpu.VMEM((N_LON * CHUNK, 8, 128), BF16),
            pltpu.VMEM((CH // GROUP, 96, 128), F32),
            pltpu.VMEM((N_LON, CHUNK, 8, 128), BF16),
            pltpu.VMEM((CHUNK, 8, 128), F32),
            pltpu.VMEM((N_LAT, CHUNK, 8, 128), F32),
            pltpu.VMEM((N_LON * CHUNK, 8, 128), BF16),
            pltpu.SemaphoreType.DMA((10,)),
            pltpu.SemaphoreType.DMA((10,)),
            pltpu.SemaphoreType.DMA((10,)),
            pltpu.SemaphoreType.DMA((2, N_LON)),
            pltpu.SemaphoreType.DMA((2, N_LON)),
            pltpu.SemaphoreType.DMA((N_LON,)),
            pltpu.SemaphoreType.DMA((N_LON,)),
            pltpu.SemaphoreType.DMA((N_LAT,)),
            pltpu.SemaphoreType.DMA((N_LAT,)),
            pltpu.SemaphoreType.DMA((N_LON,)),
            pltpu.SemaphoreType.DMA((N_LON,)),
        ],
        compiler_params=pltpu.CompilerParams(
            collective_id=0, has_side_effects=True, vmem_limit_bytes=44 * 1024 * 1024
        ),
    )(
        *(
            pltpu.with_memory_space_constraint(value, pltpu.HBM)
            for value in (
                owner.reshape(TRACKS),
                obs_count,
                footprint,
                adjoint_in,
                layer_input,
                conv_weight,
                obs_weight,
                obs_value.reshape(N_LON, 2, K, CH),
                obs_precision,
            )
        ),
    )
    return pl.pallas_call(
        unpack,
        out_shape=(
            jax.ShapeDtypeStruct((CH, ROWS, COLS), BF16),
            jax.ShapeDtypeStruct((CH // GROUP, 9, GROUP, GROUP), F32),
        ),
        in_specs=[vmem, vmem],
        out_specs=(pl.BlockSpec(memory_space=pl.ANY), pl.BlockSpec(memory_space=pl.ANY)),
        scratch_shapes=[
            pltpu.VMEM((CH // GROUP, 9, GROUP, GROUP), F32),
            pltpu.SemaphoreType.DMA((2,)),
        ],
        compiler_params=pltpu.CompilerParams(vmem_limit_bytes=8 * 1024 * 1024),
    )(field, grad)


def solution(mesh):
    in_specs = (
        P(None, "lat", "lon"),
        P(None, "lat", "lon"),
        P(),
        P(("lat", "lon"), None),
        P(("lat", "lon"), None),
        P(("lat", "lon"), None, None),
        P(("lat", "lon"), None, None),
        P(("lat", "lon"), None),
        P(("lat", "lon")),
    )
    out_specs = (P(None, "lat", "lon"), P())
    return jax.shard_map(
        on_device, mesh=mesh, in_specs=in_specs, out_specs=out_specs, check_vma=False
    )
```

```python
import math

import jax
import jax.numpy as jnp
from jax import lax
from jax.experimental import pallas as pl
from jax.experimental.pallas import tpu as pltpu
from jax.sharding import PartitionSpec as P

MESH = pl.DeviceIdType.MESH
N_LAT = 8
N_LON = 16
CH = 256
ROWS = 8
COLS = 256
CELLS = ROWS * COLS
GROUP = 32
TRACKS = 16
K = 32
PTS = 64
CHUNK = 5
CB = 64
F32 = jnp.float32
BF16 = jnp.bfloat16
NT = (((1,), (1,)), ((), ()))
STEPS = sorted(
    ((a, b) for a in range(4) for b in range(4) if a or b),
    key=lambda step: -min(step[0], 4 - step[0]) - min(step[1], 4 - step[1]),
)
PACK = 96


def iota(shape, dim):
    return lax.broadcasted_iota(jnp.int32, shape, dim)


def turn(value, shift):
    return pltpu.roll(value, shift % 128, 1) if shift % 128 else value


def kernel(
    owner_in,
    counts_in,
    fp_in,
    adj_in,
    x_in,
    conv_w,
    obs_w,
    obs_v,
    obs_p,
    out,
    grad_out,
    owner,
    counts,
    fp,
    a_nat,
    x_nat,
    f_buf,
    a_rows,
    a_shift,
    x_rows,
    x_edge,
    e_own,
    e_in,
    e_wide,
    halo_cols,
    a_edge,
    w_in,
    w_diag,
    total,
    obs_op,
    blocks,
    cell_row,
    w_nat,
    p_nat,
    packed,
    early,
    late,
    grad,
    g_acc,
    rs_buf,
    part,
    ex_buf,
    gathered,
    local_sem,
    halo_send,
    halo_recv,
    obs_send,
    obs_recv,
    rs_send,
    rs_recv,
    ex_send,
    ex_recv,
    ag_send,
    ag_recv,
):
    lat = lax.axis_index("lat")
    lon = lax.axis_index("lon")
    north = lax.rem(lat + N_LAT - 1, N_LAT)
    south = lax.rem(lat + 1, N_LAT)
    west = lax.rem(lon + N_LON - 1, N_LON)
    east = lax.rem(lon + 1, N_LON)
    outer, inner = lon // 4, lax.rem(lon, 4)
    peers = [4 * lax.rem(outer + a, 4) + lax.rem(inner + b, 4) for a, b in STEPS]

    local = [
        pltpu.make_async_copy(src, dst, local_sem.at[index])
        for index, (src, dst) in enumerate(
            (
                (adj_in, a_nat),
                (x_in, x_nat),
                (obs_w, w_nat),
                (obs_p, p_nat),
                (conv_w, w_in),
                (obs_v.at[:, 0], packed.at[:, pl.ds(0, K), :]),
                (obs_v.at[:, 1], packed.at[:, pl.ds(2 * K, K), :]),
                (owner_in, owner),
                (counts_in, counts),
                (fp_in, fp),
            )
        )
    ]
    for copy in local:
        copy.start()

    barrier = pltpu.get_barrier_semaphore()

    def greet(to_lat, to_lon):
        pl.semaphore_signal(barrier, inc=1, device_id=(to_lat, to_lon), device_id_type=MESH)

    for to_lat, to_lon in ((north, west), (north, east), (south, west), (south, east)):
        greet(to_lat, to_lon)
    for k in range(1, N_LAT):
        greet(lax.rem(lat + k, N_LAT), lon)
    for peer in peers:
        greet(lat, peer)

    lane = iota((CB, 128), 1)

    def split_rows(native, put):
        for half in range(2):
            f_buf[half] = (
                native[:, :, 128 * half : 128 * half + 128].astype(F32).reshape(CELLS, 128)
            )
        for c in range(0, CH, CB):
            first = jnp.zeros((CB, 128), F32)
            last = jnp.zeros((CB, 128), F32)
            for i in range(ROWS):
                low = f_buf[0, pl.ds(ROWS * c + i, CB, stride=ROWS), :]
                high = f_buf[1, pl.ds(ROWS * c + i, CB, stride=ROWS), :]
                here = lane // 2 == i
                first = jnp.where(here, turn(low, 2 * i), first)
                last = jnp.where(here, turn(high, 2 * i + 2), last)
                put(i, c, low, high)
            yield c, first, last

    local[0].wait()

    def put_adjoint(i, c, low, high):
        a_rows[i + 2, c : c + CB, :128] = low.astype(BF16)
        a_rows[i + 2, c : c + CB, 128:] = high.astype(BF16)

    for c, first, last in split_rows(a_nat, put_adjoint):
        halo_cols[0, c : c + CB, :] = first
        halo_cols[1, c : c + CB, :] = last
    for side in range(2):
        e_own[side] = halo_cols[side].T[: 2 * ROWS, :].astype(BF16)

    local[2].wait()
    local[3].wait()
    local[8].wait()
    obs_row = iota((K, PTS), 0)
    for s in range(2 * N_LON):
        packed[s // 2, K : 2 * K, PTS * (s % 2) : PTS * (s % 2 + 1)] = jnp.where(
            obs_row < counts[s], w_nat[s].astype(F32), 0.0
        ).astype(BF16)
        for half in range(2):
            at = K + 2 * (s % 2) + half
            packed[s // 2, at : at + 1, 128:] = p_nat[
                s : s + 1, 128 * half : 128 * half + 128
            ]
    local[5].wait()
    local[6].wait()
    early[lon] = packed[lon, : 2 * K]
    late[lon] = packed[lon, 2 * K :]

    local[1].wait()

    def put_input(i, c, low, high):
        at = slice(c, c + CB)
        low_back, high_back = turn(low, 2), turn(high, 2)
        low_on, high_on = turn(low, -2), turn(high, -2)
        x_rows[0, i, at, :128] = jnp.where(lane < 2, 0.0, low_back).astype(BF16)
        x_rows[0, i, at, 128:] = jnp.where(lane < 2, low_back, high_back).astype(BF16)
        x_rows[1, i, at, :128] = low.astype(BF16)
        x_rows[1, i, at, 128:] = high.astype(BF16)
        x_rows[2, i, at, :128] = jnp.where(lane < 126, low_on, high_on).astype(BF16)
        x_rows[2, i, at, 128:] = jnp.where(lane < 126, high_on, 0.0).astype(BF16)

    for c, first, last in split_rows(x_nat, put_input):
        x_edge[0, c : c + CB, :] = last.astype(BF16)
        x_edge[1, c : c + CB, :] = turn(first, 64).astype(BF16)

    groups = CH // GROUP

    def meeting(g, rows):
        at = slice(GROUP * g, GROUP * (g + 1))
        moved = [
            jnp.concatenate([x_rows[b, i, at, :] for b in range(3)], axis=0) for i in rows
        ]
        meets = [
            jnp.concatenate([a_rows[i + 4 - 2 * a, at, :] for a in (0, 1, 2, 2)], axis=0)
            for i in rows
        ]
        return moved, meets

    def pair_up(moved, meets):
        return lax.dot_general(
            jnp.concatenate(moved, axis=1),
            jnp.concatenate(meets, axis=1),
            NT,
            preferred_element_type=F32,
        )

    for g in range(groups):
        g_acc[g] = pair_up(*meeting(g, range(2, ROWS - 2)))

    local[4].wait()
    spread = (iota((GROUP, CH), 1) % GROUP == iota((GROUP, CH), 0)).astype(F32).astype(BF16)
    same_group = iota((CH, CH), 0) // GROUP == iota((CH, CH), 1) // GROUP
    for tap in range(9):
        stacked = jnp.concatenate([w_in[g, tap] for g in range(groups)], axis=0)
        tiled = jnp.dot(stacked, spread, preferred_element_type=F32)
        w_diag[:, CH * tap : CH * (tap + 1)] = jnp.where(same_group, tiled, 0.0).astype(BF16)

    def weigh(taps, fields):
        weights = [w_diag[:, CH * tap : CH * (tap + 1)] for tap in taps]
        return jnp.dot(
            jnp.concatenate(weights, axis=1),
            jnp.concatenate(fields, axis=0),
            preferred_element_type=F32,
        )

    def rows_of_taps(i):
        return [(a, i + 4 - 2 * a, 2 <= i + 4 - 2 * a < ROWS + 2) for a in range(3)]

    for i in range(ROWS):
        here = [(a, row) for a, row, own_row in rows_of_taps(i) if own_row]
        total[i] = a_rows[i + 2].astype(F32) + weigh(
            [3 * a + 1 for a, _ in here], [a_rows[row] for _, row in here]
        )

    pl.semaphore_wait(barrier, 4 + N_LAT - 1 + N_LON - 1)

    def halo(index, src, dst, to_lat, to_lon):
        return pltpu.make_async_remote_copy(
            src_ref=src,
            dst_ref=dst,
            send_sem=halo_send.at[index],
            recv_sem=halo_recv.at[index],
            device_id=(to_lat, to_lon),
            device_id_type=MESH,
        )

    halos = [
        halo(0, e_own.at[1], e_in.at[0], lat, east),
        halo(1, e_own.at[0], e_in.at[1], lat, west),
        halo(2, e_own.at[1], e_in.at[2], south, east),
        halo(3, e_own.at[0], e_in.at[3], south, west),
        halo(4, e_own.at[1], e_in.at[4], north, east),
        halo(5, e_own.at[0], e_in.at[5], north, west),
    ]
    for part_of in range(2):
        at = pl.ds(CH // 2 * part_of, CH // 2)
        for src, dst, to_lat in ((ROWS, 0, south), (2, ROWS + 2, north)):
            halos.append(
                halo(
                    len(halos),
                    a_rows.at[pl.ds(src, 2), at],
                    a_rows.at[pl.ds(dst, 2), at],
                    to_lat,
                    lon,
                )
            )
    for copy in halos:
        copy.start()

    def obs_copy(k, which):
        at = (pl.ds(0, 2 * K), pl.ds(2 * K, K))[which]
        return pltpu.make_async_remote_copy(
            src_ref=packed.at[peers[k], at],
            dst_ref=(early, late)[which].at[lon],
            send_sem=obs_send.at[which, k],
            recv_sem=obs_recv.at[which, k],
            device_id=(lat, peers[k]),
            device_id_type=MESH,
        )

    for k in range(N_LON - 1):
        obs_copy(k, 0).start()

    for copy in halos[:6]:
        copy.wait_recv()

    wide_lane = iota((CH, 128), 1)
    for side in range(2):
        upper = e_in[2 + side].astype(F32)[2 * ROWS - 4 :, :]
        lower = e_in[4 + side].astype(F32)[:4, :]
        e_wide[0:4, :] = jnp.where(lat > 0, upper, 0.0)
        e_wide[4 : 4 + 2 * ROWS, :] = e_in[side].astype(F32)
        e_wide[4 + 2 * ROWS : 8 + 2 * ROWS, :] = jnp.where(lat < N_LAT - 1, lower, 0.0)
        e_wide[8 + 2 * ROWS :, :] = jnp.zeros((120 - 2 * ROWS, CH), F32)
        halo_cols[side] = e_wide[...].T
    for a in range(3):
        from_east = turn(halo_cols[1], 4 * a - 8)
        from_west = turn(halo_cols[0], 64 + 4 * a - 8)
        a_edge[a] = jnp.where(wide_lane < 64, from_east, from_west).astype(BF16)

    scale = 1.0 / math.sqrt(CELLS * N_LAT * N_LON)
    nothing = jnp.zeros((GROUP, 128), BF16)
    tile_lane = iota((3 * GROUP, 128), 1)
    done = []

    def put_grad(at, value):
        grad[at : at + 12] = value.reshape(12, 8, 128).astype(BF16)

    for g in range(groups):
        if g % 4 == 0:
            half = pl.ds(CH // 2 * (g // 4), CH // 2)
            for copy in halos[6 + g // 2 : 8 + g // 2]:
                copy.wait_recv()

            @pl.when(lat == 0)
            def _(half=half):
                a_rows[0:2, half] = jnp.zeros((2, CH // 2, COLS), BF16)

            @pl.when(lat == N_LAT - 1)
            def _(half=half):
                a_rows[ROWS + 2 : ROWS + 4, half] = jnp.zeros((2, CH // 2, COLS), BF16)

        at = slice(GROUP * g, GROUP * (g + 1))
        moved, meets = meeting(g, (0, 1, ROWS - 2, ROWS - 1))
        moved.append(jnp.concatenate([x_edge[0, at, :], nothing, x_edge[1, at, :]], axis=0))
        meets.append(jnp.concatenate([a_edge[a, at, :] for a in (0, 1, 2, 2)], axis=0))
        value = (pair_up(moved, meets) + g_acc[g]) * scale
        done.append(value)
        if g % 2 == 1:
            put_grad(12 * (g // 2), jnp.where(tile_lane < 64, done[g - 1], turn(value, 64)))
        if g % 4 == 3:
            value = turn(done[g - 3], -64)
            for m in range(1, 4):
                shifted = turn(done[g - 3 + m], 32 * m - 64)
                value = jnp.where(tile_lane // GROUP == m, shifted, value)
            put_grad(48 + 12 * (g // 4), value)
    grad[72:] = jnp.zeros((8, 8, 128), BF16)

    def rs_copy(k):
        return pltpu.make_async_remote_copy(
            src_ref=grad.at[pl.ds(CHUNK * peers[k], CHUNK)],
            dst_ref=rs_buf.at[k],
            send_sem=rs_send.at[k],
            recv_sem=rs_recv.at[k],
            device_id=(lat, peers[k]),
            device_id_type=MESH,
        )

    for k in range(N_LON - 1):
        rs_copy(k).start()
    for k in range(N_LON - 1):
        obs_copy(k, 1).start()

    for row in range(ROWS + 4):
        for c in range(0, CH, CB):
            at = slice(c, c + CB)
            low = a_rows[row, at, :128].astype(F32)
            high = a_rows[row, at, 128:].astype(F32)
            low_on, high_on = turn(low, -2), turn(high, -2)
            low_back, high_back = turn(low, 2), turn(high, 2)
            east_cols = turn(halo_cols[1, at, :], 126 - 2 * row)
            west_cols = turn(halo_cols[0, at, :], -2 * row)
            a_shift[0, row, at, :128] = jnp.where(lane < 126, low_on, high_on).astype(BF16)
            a_shift[0, row, at, 128:] = jnp.where(lane < 126, high_on, east_cols).astype(BF16)
            a_shift[1, row, at, :128] = jnp.where(lane < 2, west_cols, low_back).astype(BF16)
            a_shift[1, row, at, 128:] = jnp.where(lane < 2, low_back, high_back).astype(BF16)

    for copy in (local[7], local[9]):
        copy.wait()
    for k in range(N_LON - 1):
        obs_copy(k, 0).wait_recv()
    owners = [owner[t] for t in range(TRACKS)]
    places = [
        jnp.minimum(
            sum([(owners[u] == owners[t]).astype(jnp.int32) for u in range(t)], jnp.int32(0)), 1
        )
        for t in range(TRACKS)
    ]
    cells = fp[...]
    width = COLS * N_LON
    rows_of = (cells // width - lat * ROWS).astype(F32).astype(BF16)
    cols_of = (cells % width - lon * COLS).astype(F32).astype(BF16)
    widen = (iota((PTS, 4 * PTS), 1) % PTS == iota((PTS, 4 * PTS), 0)).astype(F32).astype(BF16)
    cell = COLS * jnp.dot(rows_of, widen, preferred_element_type=F32) + jnp.dot(
        cols_of, widen, preferred_element_type=F32
    )
    widen_pair = jnp.concatenate([widen, widen], axis=0)
    slot_lane = iota((K, 2 * PTS), 1) // PTS
    own_lanes = iota((TRACKS, 4 * PTS), 1) // PTS == iota((TRACKS, 4 * PTS), 0) % 4
    cell = jnp.where(own_lanes, cell, 0.0)
    same_track = iota((4 * K, 4 * PTS), 0) // K == iota((4 * K, 4 * PTS), 1) // PTS
    for q in range(4):
        tracks = range(4 * q, 4 * q + 4)
        stacked = jnp.concatenate(
            [jnp.where(slot_lane == places[t], early[owners[t], K : 2 * K, :128].astype(F32), 0.0) for t in tracks],
            axis=0,
        )
        tiled = jnp.dot(stacked.astype(BF16), widen_pair, preferred_element_type=F32)
        blocks[q] = jnp.where(same_track, tiled, 0.0).astype(BF16)
        cell_row[q : q + 1, :] = jnp.sum(cell[4 * q : 4 * q + 4, :], axis=0, keepdims=True)

    def build_op(i, carry):
        here = (iota((COLS, 4 * PTS), 0) + i * COLS).astype(F32)
        at = pl.ds(pl.multiple_of(i * COLS, COLS), COLS)
        for q in range(4):
            hit = jnp.where(here == cell_row[q : q + 1, :], 1.0, 0.0).astype(BF16)
            obs_op[at, 4 * K * q : 4 * K * (q + 1)] = lax.dot_general(
                hit, blocks[q], NT, preferred_element_type=F32
            ).astype(BF16)
        return carry

    lax.fori_loop(0, ROWS, build_op, 0)

    own = grad[pl.ds(CHUNK * lon, CHUNK)].astype(F32)
    for k in range(N_LON - 1):
        rs_copy(k).wait_recv()
        own += rs_buf[k].astype(F32)
    part[...] = own.astype(BF16)
    ex_buf[lat] = own.astype(BF16)

    def ex_copy(k):
        return pltpu.make_async_remote_copy(
            src_ref=part,
            dst_ref=ex_buf.at[lat],
            send_sem=ex_send.at[k],
            recv_sem=ex_recv.at[k],
            device_id=(lax.rem(lat + k, N_LAT), lon),
            device_id_type=MESH,
        )

    for k in (4, 3, 5, 2, 6, 1, 7):
        ex_copy(k).start()

    model_obs = jnp.dot(
        jnp.concatenate([x_rows[1, i] for i in range(ROWS)], axis=1),
        obs_op[...],
        preferred_element_type=F32,
    ).T

    def p_row(which, place):
        rows = early[which, K : K + 4, 128:].astype(F32)
        first = jnp.concatenate([rows[0:1, :], rows[1:2, :]], axis=1)
        second = jnp.concatenate([rows[2:3, :], rows[3:4, :]], axis=1)
        return jnp.where(place == 0, first, second)

    pieces = []
    for k in range(N_LON - 1):
        obs_copy(k, 1).wait_recv()
    for t in range(TRACKS):
        value = jnp.where(
            places[t] == 0,
            early[owners[t], :K, :].astype(F32),
            late[owners[t]].astype(F32),
        )
        precision = p_row(owners[t], places[t])
        pieces.append((model_obs[K * t : K * (t + 1), :] - value) * precision)
    misfit_t = jnp.concatenate(pieces, axis=0).T.astype(BF16)

    def finish_row(i):
        taps, fields = [], []
        for a, row, own_row in rows_of_taps(i):
            taps += [3 * a, 3 * a + 2]
            fields += [a_shift[0, row], a_shift[1, row]]
            if not own_row:
                taps.append(3 * a + 1)
                fields.append(a_rows[row])
        done_row = (
            total[i]
            + weigh(taps, fields)
            + lax.dot_general(
                misfit_t,
                obs_op[COLS * i : COLS * (i + 1), :],
                NT,
                preferred_element_type=F32,
            )
        )
        for half in range(2):
            f_buf[half, pl.ds(i, CH, stride=ROWS), :] = done_row[:, 128 * half : 128 * half + 128]

    for k in range(1, N_LAT):
        ex_copy(k).wait_recv()
    whole = ex_buf[0].astype(F32)
    for k in range(1, N_LAT):
        whole += ex_buf[k].astype(F32)
    mine = pl.ds(CHUNK * lon, CHUNK)
    gathered[mine] = whole.astype(BF16)

    def ag_copy(k):
        return pltpu.make_async_remote_copy(
            src_ref=gathered.at[mine],
            dst_ref=gathered.at[mine],
            send_sem=ag_send.at[k],
            recv_sem=ag_recv.at[k],
            device_id=(lat, peers[k]),
            device_id_type=MESH,
        )

    for k in range(N_LON - 1):
        ag_copy(k).start()
    for i in range(ROWS):
        finish_row(i)
    for half in range(2):
        out[:, :, 128 * half : 128 * half + 128] = (
            f_buf[half].reshape(CH, ROWS, 128).astype(BF16)
        )

    for copy in halos:
        copy.wait_send()
    for k in range(1, N_LAT):
        ex_copy(k).wait_send()
    for k in range(N_LON - 1):
        obs_copy(k, 0).wait_send()
        obs_copy(k, 1).wait_send()
        rs_copy(k).wait_send()
        ag_copy(k).wait_send()
    for k in range(N_LON - 1):
        ag_copy(k).wait_recv()
    grad_out[...] = gathered[...]


def unpack(field, grad, out, grad_out, blocks, sem):
    copy = pltpu.make_async_copy(field, out, sem.at[0])
    copy.start()
    for g in range(CH // GROUP):
        for a in range(3):
            if a < 2:
                at, shift = 12 * (g // 2), 64 * (g % 2) + GROUP * a
            else:
                at, shift = 48 + 12 * (g // 4), GROUP * (g % 4)
            value = turn(grad[at : at + 12].astype(F32).reshape(96, 128), -shift)[:, :GROUP]
            for b in range(3):
                blocks[g, 3 * a + b] = value[GROUP * b : GROUP * (b + 1), :]
    copy_grad = pltpu.make_async_copy(blocks, grad_out, sem.at[1])
    copy_grad.start()
    copy.wait()
    copy_grad.wait()


def on_device(
    adjoint_in,
    layer_input,
    conv_weight,
    footprint,
    owner,
    obs_weight,
    obs_value,
    obs_precision,
    obs_count,
):
    anywhere = pl.BlockSpec(memory_space=pltpu.HBM)
    vmem = pl.BlockSpec(memory_space=pltpu.VMEM)
    field, grad = pl.pallas_call(
        kernel,
        out_shape=(
            jax.ShapeDtypeStruct((CH, ROWS, COLS), BF16),
            jax.ShapeDtypeStruct((N_LON * CHUNK, 8, 128), BF16),
        ),
        in_specs=[anywhere] * 9,
        out_specs=(vmem, vmem),
        scratch_shapes=[
            pltpu.SMEM((TRACKS,), jnp.int32),
            pltpu.SMEM((2 * N_LON,), jnp.int32),
            pltpu.VMEM((TRACKS, PTS), jnp.int32),
            pltpu.VMEM((CH, ROWS, COLS), BF16),
            pltpu.VMEM((CH, ROWS, COLS), BF16),
            pltpu.VMEM((2, CELLS, 128), F32),
            pltpu.VMEM((ROWS + 4, CH, COLS), BF16),
            pltpu.VMEM((2, ROWS + 4, CH, COLS), BF16),
            pltpu.VMEM((3, ROWS, CH, COLS), BF16),
            pltpu.VMEM((2, CH, 128), BF16),
            pltpu.VMEM((2, 2 * ROWS, CH), BF16),
            pltpu.VMEM((6, 2 * ROWS, CH), BF16),
            pltpu.VMEM((128, CH), F32),
            pltpu.VMEM((2, CH, 128), F32),
            pltpu.VMEM((3, CH, 128), BF16),
            pltpu.VMEM((CH // GROUP, 9, GROUP, GROUP), BF16),
            pltpu.VMEM((CH, 9 * CH), BF16),
            pltpu.VMEM((ROWS, CH, COLS), F32),
            pltpu.VMEM((CELLS, TRACKS * K), BF16),
            pltpu.VMEM((4, 4 * K, 4 * PTS), BF16),
            pltpu.VMEM((8, 4 * PTS), F32),
            pltpu.VMEM((2 * N_LON, K, PTS), BF16),
            pltpu.VMEM((2 * N_LON, CH), BF16),
            pltpu.VMEM((N_LON, PACK, CH), BF16),
            pltpu.VMEM((N_LON, 2 * K, CH), BF16),
            pltpu.VMEM((N_LON, K, CH), BF16),
            pltpu.VMEM((N_LON * CHUNK, 8, 128), BF16),
            pltpu.VMEM((CH // GROUP, 96, 128), F32),
            pltpu.VMEM((N_LON, CHUNK, 8, 128), BF16),
            pltpu.VMEM((CHUNK, 8, 128), BF16),
            pltpu.VMEM((N_LAT, CHUNK, 8, 128), BF16),
            pltpu.VMEM((N_LON * CHUNK, 8, 128), BF16),
            pltpu.SemaphoreType.DMA((10,)),
            pltpu.SemaphoreType.DMA((10,)),
            pltpu.SemaphoreType.DMA((10,)),
            pltpu.SemaphoreType.DMA((2, N_LON)),
            pltpu.SemaphoreType.DMA((2, N_LON)),
            pltpu.SemaphoreType.DMA((N_LON,)),
            pltpu.SemaphoreType.DMA((N_LON,)),
            pltpu.SemaphoreType.DMA((N_LAT,)),
            pltpu.SemaphoreType.DMA((N_LAT,)),
            pltpu.SemaphoreType.DMA((N_LON,)),
            pltpu.SemaphoreType.DMA((N_LON,)),
        ],
        compiler_params=pltpu.CompilerParams(
            collective_id=0, has_side_effects=True, vmem_limit_bytes=44 * 1024 * 1024
        ),
    )(
        *(
            pltpu.with_memory_space_constraint(value, pltpu.HBM)
            for value in (
                owner.reshape(TRACKS),
                obs_count,
                footprint,
                adjoint_in,
                layer_input,
                conv_weight,
                obs_weight,
                obs_value.reshape(N_LON, 2, K, CH),
                obs_precision,
            )
        ),
    )
    return pl.pallas_call(
        unpack,
        out_shape=(
            jax.ShapeDtypeStruct((CH, ROWS, COLS), BF16),
            jax.ShapeDtypeStruct((CH // GROUP, 9, GROUP, GROUP), F32),
        ),
        in_specs=[vmem, vmem],
        out_specs=(pl.BlockSpec(memory_space=pl.ANY), pl.BlockSpec(memory_space=pl.ANY)),
        scratch_shapes=[
            pltpu.VMEM((CH // GROUP, 9, GROUP, GROUP), F32),
            pltpu.SemaphoreType.DMA((2,)),
        ],
        compiler_params=pltpu.CompilerParams(vmem_limit_bytes=8 * 1024 * 1024),
    )(field, grad)


def solution(mesh):
    in_specs = (
        P(None, "lat", "lon"),
        P(None, "lat", "lon"),
        P(),
        P(("lat", "lon"), None),
        P(("lat", "lon"), None),
        P(("lat", "lon"), None, None),
        P(("lat", "lon"), None, None),
        P(("lat", "lon"), None),
        P(("lat", "lon")),
    )
    out_specs = (P(None, "lat", "lon"), P())
    return jax.shard_map(
        on_device, mesh=mesh, in_specs=in_specs, out_specs=out_specs, check_vma=False
    )
```

```python
import math

import jax
import jax.numpy as jnp
from jax import lax
from jax.experimental import pallas as pl
from jax.experimental.pallas import tpu as pltpu
from jax.sharding import PartitionSpec as P

MESH = pl.DeviceIdType.MESH
N_LAT = 8
N_LON = 16
CH = 256
ROWS = 8
COLS = 256
CELLS = ROWS * COLS
GROUP = 32
TRACKS = 16
K = 32
PTS = 64
CHUNK = 5
CB = 64
F32 = jnp.float32
BF16 = jnp.bfloat16
NT = (((1,), (1,)), ((), ()))
STEPS = sorted(
    ((a, b) for a in range(4) for b in range(4) if a or b),
    key=lambda step: -min(step[0], 4 - step[0]) - min(step[1], 4 - step[1]),
)
PACK = 96


def iota(shape, dim):
    return lax.broadcasted_iota(jnp.int32, shape, dim)


def turn(value, shift):
    return pltpu.roll(value, shift % 128, 1) if shift % 128 else value


def kernel(
    owner_in,
    counts_in,
    fp_in,
    adj_in,
    x_in,
    conv_w,
    obs_w,
    obs_v,
    obs_p,
    out,
    grad_out,
    owner,
    counts,
    fp,
    a_nat,
    x_nat,
    f_buf,
    a_rows,
    a_shift,
    x_rows,
    x_edge,
    e_own,
    e_in,
    e_wide,
    halo_cols,
    a_edge,
    w_in,
    w_diag,
    total,
    obs_op,
    blocks,
    cell_row,
    w_nat,
    p_nat,
    packed,
    early,
    late,
    grad,
    g_acc,
    rs_buf,
    part,
    ex_buf,
    gathered,
    local_sem,
    halo_send,
    halo_recv,
    obs_send,
    obs_recv,
    rs_send,
    rs_recv,
    ex_send,
    ex_recv,
    ag_send,
    ag_recv,
):
    lat = lax.axis_index("lat")
    lon = lax.axis_index("lon")
    north = lax.rem(lat + N_LAT - 1, N_LAT)
    south = lax.rem(lat + 1, N_LAT)
    west = lax.rem(lon + N_LON - 1, N_LON)
    east = lax.rem(lon + 1, N_LON)
    outer, inner = lon // 4, lax.rem(lon, 4)
    peers = [4 * lax.rem(outer + a, 4) + lax.rem(inner + b, 4) for a, b in STEPS]

    local = [
        pltpu.make_async_copy(src, dst, local_sem.at[index])
        for index, (src, dst) in enumerate(
            (
                (adj_in, a_nat),
                (x_in, x_nat),
                (obs_w, w_nat),
                (obs_p, p_nat),
                (conv_w, w_in),
                (obs_v.at[:, 0], packed.at[:, pl.ds(0, K), :]),
                (obs_v.at[:, 1], packed.at[:, pl.ds(2 * K, K), :]),
                (owner_in, owner),
                (counts_in, counts),
                (fp_in, fp),
            )
        )
    ]
    for copy in local:
        copy.start()

    barrier = pltpu.get_barrier_semaphore()

    def greet(to_lat, to_lon):
        pl.semaphore_signal(barrier, inc=1, device_id=(to_lat, to_lon), device_id_type=MESH)

    for to_lat, to_lon in ((north, west), (north, east), (south, west), (south, east)):
        greet(to_lat, to_lon)
    for k in range(1, N_LAT):
        greet(lax.rem(lat + k, N_LAT), lon)
    for peer in peers:
        greet(lat, peer)

    lane = iota((CB, 128), 1)

    def split_rows(native, put):
        for half in range(2):
            f_buf[half] = (
                native[:, :, 128 * half : 128 * half + 128].astype(F32).reshape(CELLS, 128)
            )
        for c in range(0, CH, CB):
            first = jnp.zeros((CB, 128), F32)
            last = jnp.zeros((CB, 128), F32)
            for i in range(ROWS):
                low = f_buf[0, pl.ds(ROWS * c + i, CB, stride=ROWS), :]
                high = f_buf[1, pl.ds(ROWS * c + i, CB, stride=ROWS), :]
                here = lane // 2 == i
                first = jnp.where(here, turn(low, 2 * i), first)
                last = jnp.where(here, turn(high, 2 * i + 2), last)
                put(i, c, low, high)
            yield c, first, last

    local[0].wait()

    def put_adjoint(i, c, low, high):
        a_rows[i + 2, c : c + CB, :128] = low.astype(BF16)
        a_rows[i + 2, c : c + CB, 128:] = high.astype(BF16)

    for c, first, last in split_rows(a_nat, put_adjoint):
        halo_cols[0, c : c + CB, :] = first
        halo_cols[1, c : c + CB, :] = last
    for side in range(2):
        e_own[side] = halo_cols[side].T[: 2 * ROWS, :].astype(BF16)

    local[2].wait()
    local[3].wait()
    local[8].wait()
    obs_row = iota((K, PTS), 0)
    for s in range(2 * N_LON):
        packed[s // 2, K : 2 * K, PTS * (s % 2) : PTS * (s % 2 + 1)] = jnp.where(
            obs_row < counts[s], w_nat[s].astype(F32), 0.0
        ).astype(BF16)
        for half in range(2):
            at = K + 2 * (s % 2) + half
            packed[s // 2, at : at + 1, 128:] = p_nat[
                s : s + 1, 128 * half : 128 * half + 128
            ]
    local[5].wait()
    local[6].wait()
    early[lon] = packed[lon, : 2 * K]
    late[lon] = packed[lon, 2 * K :]

    local[1].wait()

    def put_input(i, c, low, high):
        at = slice(c, c + CB)
        low_back, high_back = turn(low, 2), turn(high, 2)
        low_on, high_on = turn(low, -2), turn(high, -2)
        x_rows[0, i, at, :128] = jnp.where(lane < 2, 0.0, low_back).astype(BF16)
        x_rows[0, i, at, 128:] = jnp.where(lane < 2, low_back, high_back).astype(BF16)
        x_rows[1, i, at, :128] = low.astype(BF16)
        x_rows[1, i, at, 128:] = high.astype(BF16)
        x_rows[2, i, at, :128] = jnp.where(lane < 126, low_on, high_on).astype(BF16)
        x_rows[2, i, at, 128:] = jnp.where(lane < 126, high_on, 0.0).astype(BF16)

    for c, first, last in split_rows(x_nat, put_input):
        x_edge[0, c : c + CB, :] = last.astype(BF16)
        x_edge[1, c : c + CB, :] = turn(first, 64).astype(BF16)

    groups = CH // GROUP

    def meeting(g, rows):
        at = slice(GROUP * g, GROUP * (g + 1))
        moved = [
            jnp.concatenate([x_rows[b, i, at, :] for b in range(3)], axis=0) for i in rows
        ]
        meets = [
            jnp.concatenate([a_rows[i + 4 - 2 * a, at, :] for a in (0, 1, 2, 2)], axis=0)
            for i in rows
        ]
        return moved, meets

    def pair_up(moved, meets):
        return lax.dot_general(
            jnp.concatenate(moved, axis=1),
            jnp.concatenate(meets, axis=1),
            NT,
            preferred_element_type=F32,
        )

    for g in range(groups):
        g_acc[g] = pair_up(*meeting(g, range(2, ROWS - 2)))

    local[4].wait()
    spread = (iota((GROUP, CH), 1) % GROUP == iota((GROUP, CH), 0)).astype(F32).astype(BF16)
    same_group = iota((CH, CH), 0) // GROUP == iota((CH, CH), 1) // GROUP
    for tap in range(9):
        stacked = jnp.concatenate([w_in[g, tap] for g in range(groups)], axis=0)
        tiled = jnp.dot(stacked, spread, preferred_element_type=F32)
        w_diag[:, CH * tap : CH * (tap + 1)] = jnp.where(same_group, tiled, 0.0).astype(BF16)

    def weigh(taps, fields):
        weights = [w_diag[:, CH * tap : CH * (tap + 1)] for tap in taps]
        return jnp.dot(
            jnp.concatenate(weights, axis=1),
            jnp.concatenate(fields, axis=0),
            preferred_element_type=F32,
        )

    def rows_of_taps(i):
        return [(a, i + 4 - 2 * a, 2 <= i + 4 - 2 * a < ROWS + 2) for a in range(3)]

    for i in range(ROWS):
        here = [(a, row) for a, row, own_row in rows_of_taps(i) if own_row]
        total[i] = a_rows[i + 2].astype(F32) + weigh(
            [3 * a + 1 for a, _ in here], [a_rows[row] for _, row in here]
        )

    pl.semaphore_wait(barrier, 4 + N_LAT - 1 + N_LON - 1)

    def halo(index, src, dst, to_lat, to_lon):
        return pltpu.make_async_remote_copy(
            src_ref=src,
            dst_ref=dst,
            send_sem=halo_send.at[index],
            recv_sem=halo_recv.at[index],
            device_id=(to_lat, to_lon),
            device_id_type=MESH,
        )

    halos = [
        halo(0, e_own.at[1], e_in.at[0], lat, east),
        halo(1, e_own.at[0], e_in.at[1], lat, west),
        halo(2, e_own.at[1], e_in.at[2], south, east),
        halo(3, e_own.at[0], e_in.at[3], south, west),
        halo(4, e_own.at[1], e_in.at[4], north, east),
        halo(5, e_own.at[0], e_in.at[5], north, west),
    ]
    for part_of in range(2):
        at = pl.ds(CH // 2 * part_of, CH // 2)
        for src, dst, to_lat in ((ROWS, 0, south), (2, ROWS + 2, north)):
            halos.append(
                halo(
                    len(halos),
                    a_rows.at[pl.ds(src, 2), at],
                    a_rows.at[pl.ds(dst, 2), at],
                    to_lat,
                    lon,
                )
            )
    for copy in halos:
        copy.start()

    def obs_copy(k, which):
        at = (pl.ds(0, 2 * K), pl.ds(2 * K, K))[which]
        return pltpu.make_async_remote_copy(
            src_ref=packed.at[peers[k], at],
            dst_ref=(early, late)[which].at[lon],
            send_sem=obs_send.at[which, k],
            recv_sem=obs_recv.at[which, k],
            device_id=(lat, peers[k]),
            device_id_type=MESH,
        )

    for k in range(N_LON - 1):
        obs_copy(k, 0).start()

    for copy in halos[:6]:
        copy.wait_recv()

    wide_lane = iota((CH, 128), 1)
    for side in range(2):
        upper = e_in[2 + side].astype(F32)[2 * ROWS - 4 :, :]
        lower = e_in[4 + side].astype(F32)[:4, :]
        e_wide[0:4, :] = jnp.where(lat > 0, upper, 0.0)
        e_wide[4 : 4 + 2 * ROWS, :] = e_in[side].astype(F32)
        e_wide[4 + 2 * ROWS : 8 + 2 * ROWS, :] = jnp.where(lat < N_LAT - 1, lower, 0.0)
        e_wide[8 + 2 * ROWS :, :] = jnp.zeros((120 - 2 * ROWS, CH), F32)
        halo_cols[side] = e_wide[...].T
    for a in range(3):
        from_east = turn(halo_cols[1], 4 * a - 8)
        from_west = turn(halo_cols[0], 64 + 4 * a - 8)
        a_edge[a] = jnp.where(wide_lane < 64, from_east, from_west).astype(BF16)

    scale = 1.0 / math.sqrt(CELLS * N_LAT * N_LON)
    nothing = jnp.zeros((GROUP, 128), BF16)
    tile_lane = iota((3 * GROUP, 128), 1)
    done = []

    def put_grad(at, value):
        grad[at : at + 12] = value.reshape(12, 8, 128).astype(BF16)

    for g in range(groups):
        if g % 4 == 0:
            half = pl.ds(CH // 2 * (g // 4), CH // 2)
            for copy in halos[6 + g // 2 : 8 + g // 2]:
                copy.wait_recv()

            @pl.when(lat == 0)
            def _(half=half):
                a_rows[0:2, half] = jnp.zeros((2, CH // 2, COLS), BF16)

            @pl.when(lat == N_LAT - 1)
            def _(half=half):
                a_rows[ROWS + 2 : ROWS + 4, half] = jnp.zeros((2, CH // 2, COLS), BF16)

        at = slice(GROUP * g, GROUP * (g + 1))
        moved, meets = meeting(g, (0, 1, ROWS - 2, ROWS - 1))
        moved.append(jnp.concatenate([x_edge[0, at, :], nothing, x_edge[1, at, :]], axis=0))
        meets.append(jnp.concatenate([a_edge[a, at, :] for a in (0, 1, 2, 2)], axis=0))
        value = (pair_up(moved, meets) + g_acc[g]) * scale
        done.append(value)
        if g % 2 == 1:
            put_grad(12 * (g // 2), jnp.where(tile_lane < 64, done[g - 1], turn(value, 64)))
        if g % 4 == 3:
            value = turn(done[g - 3], -64)
            for m in range(1, 4):
                shifted = turn(done[g - 3 + m], 32 * m - 64)
                value = jnp.where(tile_lane // GROUP == m, shifted, value)
            put_grad(48 + 12 * (g // 4), value)
    grad[72:] = jnp.zeros((8, 8, 128), BF16)

    def rs_copy(k):
        return pltpu.make_async_remote_copy(
            src_ref=grad.at[pl.ds(CHUNK * peers[k], CHUNK)],
            dst_ref=rs_buf.at[k],
            send_sem=rs_send.at[k],
            recv_sem=rs_recv.at[k],
            device_id=(lat, peers[k]),
            device_id_type=MESH,
        )

    for k in range(N_LON - 1):
        rs_copy(k).start()
    for k in range(N_LON - 1):
        obs_copy(k, 1).start()

    for row in range(ROWS + 4):
        for c in range(0, CH, CB):
            at = slice(c, c + CB)
            low = a_rows[row, at, :128].astype(F32)
            high = a_rows[row, at, 128:].astype(F32)
            low_on, high_on = turn(low, -2), turn(high, -2)
            low_back, high_back = turn(low, 2), turn(high, 2)
            east_cols = turn(halo_cols[1, at, :], 126 - 2 * row)
            west_cols = turn(halo_cols[0, at, :], -2 * row)
            a_shift[0, row, at, :128] = jnp.where(lane < 126, low_on, high_on).astype(BF16)
            a_shift[0, row, at, 128:] = jnp.where(lane < 126, high_on, east_cols).astype(BF16)
            a_shift[1, row, at, :128] = jnp.where(lane < 2, west_cols, low_back).astype(BF16)
            a_shift[1, row, at, 128:] = jnp.where(lane < 2, low_back, high_back).astype(BF16)

    for copy in (local[7], local[9]):
        copy.wait()
    for k in range(N_LON - 1):
        obs_copy(k, 0).wait_recv()
    owners = [owner[t] for t in range(TRACKS)]
    places = [
        jnp.minimum(
            sum([(owners[u] == owners[t]).astype(jnp.int32) for u in range(t)], jnp.int32(0)), 1
        )
        for t in range(TRACKS)
    ]
    cells = fp[...]
    width = COLS * N_LON
    rows_of = (cells // width - lat * ROWS).astype(F32).astype(BF16)
    cols_of = (cells % width - lon * COLS).astype(F32).astype(BF16)
    widen = (iota((PTS, 4 * PTS), 1) % PTS == iota((PTS, 4 * PTS), 0)).astype(F32).astype(BF16)
    cell = COLS * jnp.dot(rows_of, widen, preferred_element_type=F32) + jnp.dot(
        cols_of, widen, preferred_element_type=F32
    )
    widen_pair = jnp.concatenate([widen, widen], axis=0)
    slot_lane = iota((K, 2 * PTS), 1) // PTS
    own_lanes = iota((TRACKS, 4 * PTS), 1) // PTS == iota((TRACKS, 4 * PTS), 0) % 4
    cell = jnp.where(own_lanes, cell, 0.0)
    same_track = iota((4 * K, 4 * PTS), 0) // K == iota((4 * K, 4 * PTS), 1) // PTS
    for q in range(4):
        tracks = range(4 * q, 4 * q + 4)
        stacked = jnp.concatenate(
            [jnp.where(slot_lane == places[t], early[owners[t], K : 2 * K, :128].astype(F32), 0.0) for t in tracks],
            axis=0,
        )
        tiled = jnp.dot(stacked.astype(BF16), widen_pair, preferred_element_type=F32)
        blocks[q] = jnp.where(same_track, tiled, 0.0).astype(BF16)
        cell_row[q : q + 1, :] = jnp.sum(cell[4 * q : 4 * q + 4, :], axis=0, keepdims=True)

    def build_op(i, carry):
        here = (iota((COLS, 4 * PTS), 0) + i * COLS).astype(F32)
        at = pl.ds(pl.multiple_of(i * COLS, COLS), COLS)
        for q in range(4):
            hit = jnp.where(here == cell_row[q : q + 1, :], 1.0, 0.0).astype(BF16)
            obs_op[at, 4 * K * q : 4 * K * (q + 1)] = lax.dot_general(
                hit, blocks[q], NT, preferred_element_type=F32
            ).astype(BF16)
        return carry

    lax.fori_loop(0, ROWS, build_op, 0)

    own = grad[pl.ds(CHUNK * lon, CHUNK)].astype(F32)
    for k in range(N_LON - 1):
        rs_copy(k).wait_recv()
        own += rs_buf[k].astype(F32)
    part[...] = own
    ex_buf[lat] = own

    def ex_copy(k):
        return pltpu.make_async_remote_copy(
            src_ref=part,
            dst_ref=ex_buf.at[lat],
            send_sem=ex_send.at[k],
            recv_sem=ex_recv.at[k],
            device_id=(lax.rem(lat + k, N_LAT), lon),
            device_id_type=MESH,
        )

    for k in (4, 3, 5, 2, 6, 1, 7):
        ex_copy(k).start()

    model_obs = jnp.dot(
        jnp.concatenate([x_rows[1, i] for i in range(ROWS)], axis=1),
        obs_op[...],
        preferred_element_type=F32,
    ).T

    for k in range(1, N_LAT):
        ex_copy(k).wait_recv()
    whole = ex_buf[0]
    for k in range(1, N_LAT):
        whole += ex_buf[k]
    mine = pl.ds(CHUNK * lon, CHUNK)
    gathered[mine] = whole.astype(BF16)

    def ag_copy(k):
        return pltpu.make_async_remote_copy(
            src_ref=gathered.at[mine],
            dst_ref=gathered.at[mine],
            send_sem=ag_send.at[k],
            recv_sem=ag_recv.at[k],
            device_id=(lat, peers[k]),
            device_id_type=MESH,
        )

    for k in range(N_LON - 1):
        ag_copy(k).start()

    def p_row(which, place):
        rows = early[which, K : K + 4, 128:].astype(F32)
        first = jnp.concatenate([rows[0:1, :], rows[1:2, :]], axis=1)
        second = jnp.concatenate([rows[2:3, :], rows[3:4, :]], axis=1)
        return jnp.where(place == 0, first, second)

    pieces = []
    for k in range(N_LON - 1):
        obs_copy(k, 1).wait_recv()
    for t in range(TRACKS):
        value = jnp.where(
            places[t] == 0,
            early[owners[t], :K, :].astype(F32),
            late[owners[t]].astype(F32),
        )
        precision = p_row(owners[t], places[t])
        pieces.append((model_obs[K * t : K * (t + 1), :] - value) * precision)
    misfit_t = jnp.concatenate(pieces, axis=0).T.astype(BF16)

    def finish_row(i):
        taps, fields = [], []
        for a, row, own_row in rows_of_taps(i):
            taps += [3 * a, 3 * a + 2]
            fields += [a_shift[0, row], a_shift[1, row]]
            if not own_row:
                taps.append(3 * a + 1)
                fields.append(a_rows[row])
        done_row = (
            total[i]
            + weigh(taps, fields)
            + lax.dot_general(
                misfit_t,
                obs_op[COLS * i : COLS * (i + 1), :],
                NT,
                preferred_element_type=F32,
            )
        )
        for half in range(2):
            f_buf[half, pl.ds(i, CH, stride=ROWS), :] = done_row[:, 128 * half : 128 * half + 128]

    for i in range(ROWS):
        finish_row(i)
    for half in range(2):
        out[:, :, 128 * half : 128 * half + 128] = (
            f_buf[half].reshape(CH, ROWS, 128).astype(BF16)
        )

    for copy in halos:
        copy.wait_send()
    for k in range(1, N_LAT):
        ex_copy(k).wait_send()
    for k in range(N_LON - 1):
        obs_copy(k, 0).wait_send()
        obs_copy(k, 1).wait_send()
        rs_copy(k).wait_send()
        ag_copy(k).wait_send()
    for k in range(N_LON - 1):
        ag_copy(k).wait_recv()
    grad_out[...] = gathered[...]


def unpack(field, grad, out, grad_out, blocks, sem):
    copy = pltpu.make_async_copy(field, out, sem.at[0])
    copy.start()
    for g in range(CH // GROUP):
        for a in range(3):
            if a < 2:
                at, shift = 12 * (g // 2), 64 * (g % 2) + GROUP * a
            else:
                at, shift = 48 + 12 * (g // 4), GROUP * (g % 4)
            value = turn(grad[at : at + 12].astype(F32).reshape(96, 128), -shift)[:, :GROUP]
            for b in range(3):
                blocks[g, 3 * a + b] = value[GROUP * b : GROUP * (b + 1), :]
    copy_grad = pltpu.make_async_copy(blocks, grad_out, sem.at[1])
    copy_grad.start()
    copy.wait()
    copy_grad.wait()


def on_device(
    adjoint_in,
    layer_input,
    conv_weight,
    footprint,
    owner,
    obs_weight,
    obs_value,
    obs_precision,
    obs_count,
):
    anywhere = pl.BlockSpec(memory_space=pltpu.HBM)
    vmem = pl.BlockSpec(memory_space=pltpu.VMEM)
    field, grad = pl.pallas_call(
        kernel,
        out_shape=(
            jax.ShapeDtypeStruct((CH, ROWS, COLS), BF16),
            jax.ShapeDtypeStruct((N_LON * CHUNK, 8, 128), BF16),
        ),
        in_specs=[anywhere] * 9,
        out_specs=(vmem, vmem),
        scratch_shapes=[
            pltpu.SMEM((TRACKS,), jnp.int32),
            pltpu.SMEM((2 * N_LON,), jnp.int32),
            pltpu.VMEM((TRACKS, PTS), jnp.int32),
            pltpu.VMEM((CH, ROWS, COLS), BF16),
            pltpu.VMEM((CH, ROWS, COLS), BF16),
            pltpu.VMEM((2, CELLS, 128), F32),
            pltpu.VMEM((ROWS + 4, CH, COLS), BF16),
            pltpu.VMEM((2, ROWS + 4, CH, COLS), BF16),
            pltpu.VMEM((3, ROWS, CH, COLS), BF16),
            pltpu.VMEM((2, CH, 128), BF16),
            pltpu.VMEM((2, 2 * ROWS, CH), BF16),
            pltpu.VMEM((6, 2 * ROWS, CH), BF16),
            pltpu.VMEM((128, CH), F32),
            pltpu.VMEM((2, CH, 128), F32),
            pltpu.VMEM((3, CH, 128), BF16),
            pltpu.VMEM((CH // GROUP, 9, GROUP, GROUP), BF16),
            pltpu.VMEM((CH, 9 * CH), BF16),
            pltpu.VMEM((ROWS, CH, COLS), F32),
            pltpu.VMEM((CELLS, TRACKS * K), BF16),
            pltpu.VMEM((4, 4 * K, 4 * PTS), BF16),
            pltpu.VMEM((8, 4 * PTS), F32),
            pltpu.VMEM((2 * N_LON, K, PTS), BF16),
            pltpu.VMEM((2 * N_LON, CH), BF16),
            pltpu.VMEM((N_LON, PACK, CH), BF16),
            pltpu.VMEM((N_LON, 2 * K, CH), BF16),
            pltpu.VMEM((N_LON, K, CH), BF16),
            pltpu.VMEM((N_LON * CHUNK, 8, 128), BF16),
            pltpu.VMEM((CH // GROUP, 96, 128), F32),
            pltpu.VMEM((N_LON, CHUNK, 8, 128), BF16),
            pltpu.VMEM((CHUNK, 8, 128), F32),
            pltpu.VMEM((N_LAT, CHUNK, 8, 128), F32),
            pltpu.VMEM((N_LON * CHUNK, 8, 128), BF16),
            pltpu.SemaphoreType.DMA((10,)),
            pltpu.SemaphoreType.DMA((10,)),
            pltpu.SemaphoreType.DMA((10,)),
            pltpu.SemaphoreType.DMA((2, N_LON)),
            pltpu.SemaphoreType.DMA((2, N_LON)),
            pltpu.SemaphoreType.DMA((N_LON,)),
            pltpu.SemaphoreType.DMA((N_LON,)),
            pltpu.SemaphoreType.DMA((N_LAT,)),
            pltpu.SemaphoreType.DMA((N_LAT,)),
            pltpu.SemaphoreType.DMA((N_LON,)),
            pltpu.SemaphoreType.DMA((N_LON,)),
        ],
        compiler_params=pltpu.CompilerParams(
            collective_id=0, has_side_effects=True, vmem_limit_bytes=44 * 1024 * 1024
        ),
    )(
        *(
            pltpu.with_memory_space_constraint(value, pltpu.HBM)
            for value in (
                owner.reshape(TRACKS),
                obs_count,
                footprint,
                adjoint_in,
                layer_input,
                conv_weight,
                obs_weight,
                obs_value.reshape(N_LON, 2, K, CH),
                obs_precision,
            )
        ),
    )
    return pl.pallas_call(
        unpack,
        out_shape=(
            jax.ShapeDtypeStruct((CH, ROWS, COLS), BF16),
            jax.ShapeDtypeStruct((CH // GROUP, 9, GROUP, GROUP), F32),
        ),
        in_specs=[vmem, vmem],
        out_specs=(pl.BlockSpec(memory_space=pl.ANY), pl.BlockSpec(memory_space=pl.ANY)),
        scratch_shapes=[
            pltpu.VMEM((CH // GROUP, 9, GROUP, GROUP), F32),
            pltpu.SemaphoreType.DMA((2,)),
        ],
        compiler_params=pltpu.CompilerParams(vmem_limit_bytes=8 * 1024 * 1024),
    )(field, grad)


def solution(mesh):
    in_specs = (
        P(None, "lat", "lon"),
        P(None, "lat", "lon"),
        P(),
        P(("lat", "lon"), None),
        P(("lat", "lon"), None),
        P(("lat", "lon"), None, None),
        P(("lat", "lon"), None, None),
        P(("lat", "lon"), None),
        P(("lat", "lon")),
    )
    out_specs = (P(None, "lat", "lon"), P())
    return jax.shard_map(
        on_device, mesh=mesh, in_specs=in_specs, out_specs=out_specs, check_vma=False
    )
```
